32 devices in a mesh: section: 2 (over core), expert: 4 (over z), tensor: 4 (over y, x).
Axes of the slice: x: 2, y: 2, z: 4, core: 2. Of those that a mesh axis runs over, the one named last changes fastest.
Arguments:
- tokens: bfloat16 [32, 197, 768], P('expert'), may hold values from -6 to 6
- batch_order: int32 [4, 8], P('expert'), may hold values from 0 to 7, each once within a row
- gain_attn: float32 [2, 768], P('section'), may hold values from 0.5 to 1.5
- shift_attn: float32 [2, 768], P('section'), may hold values from -3 to 3
- w_qkv: bfloat16 [2, 3, 768, 768], P('section', None, None, 'tensor'), may hold values from -0.21650635 to 0.21650635
- w_out: bfloat16 [2, 768, 768], P('section', 'tensor'), may hold values from -0.875 to 0.875
- gain_moe: float32 [2, 768], P('section'), may hold values from 0.5 to 1.5
- shift_moe: float32 [2, 768], P('section'), may hold values from -3 to 3
- w_router: float32 [2, 768, 8], P('section'), may hold values from -0.04330127 to 0.04330127
- w_in: bfloat16 [2, 8, 768, 3072], P('section', 'expert', None, 'tensor'), may hold values from -0.21875 to 0.21875
- w_back: bfloat16 [2, 8, 3072, 768], P('section', 'expert', 'tensor'), may hold values from -0.4375 to 0.4375
- routes: int32 [2, 32, 197, 2], P('section', 'expert'), may hold values from 0 to 7, as said below
- slots: int32 [2, 32, 197, 2], P('section', 'expert'), may hold values from -1 to 127, as said below
- cotangent: bfloat16 [32, 197, 768], P('expert'), may hold values from -6 to 6
Outputs:
- acts: bfloat16 [2, 32, 197, 768], P('section', 'expert')
- in_grads: float32 [2, 32, 197, 768], P('section', 'expert')
- grad_gain_attn: float32 [2, 768], P('section')
- grad_shift_attn: float32 [2, 768], P('section')
- grad_qkv: float32 [2, 3, 768, 768], P('section', None, None, 'tensor')
- grad_out: float32 [2, 768, 768], P('section', 'tensor')
- grad_gain_moe: float32 [2, 768], P('section')
- grad_shift_moe: float32 [2, 768], P('section')
- grad_router: float32 [2, 768, 8], P('section')
- grad_in: float32 [2, 8, 768, 3072], P('section', 'expert', None, 'tensor')
- grad_back: float32 [2, 8, 3072, 768], P('section', 'expert', 'tensor')
The draws below stay inside these ranges and needn't reach their ends.
Inputs may be any that keep to these rules, and one draw needn't show every extreme that they name: `routes`: the two experts of a token differ. `slots`: within one layer and one block, choices are ranked first choices by row, then second choices by row, per expert; a choice's slot is its rank, -1 from rank 128 on.
All inputs are finite; a program needn't handle non-finite values.
Results may differ from the reference program's by a relative error of at most 0.019.
Values may be sent and summed in bfloat16 or wider, within the bound.
No kernel may reach another device: no remote copies, remote signals or barrier semaphores. Data moves between devices by JAX's collectives and lax.ppermute only.
A program may use at most 256 MiB of HBM per device.

```python
import jax
import jax.numpy as jnp
from jax import lax

D = 768
HEADS = 12
HEAD = 64
FF = 3072
TOPK = 2
SEQ = 197
MB = 4
IMG_MB = 2
SECTIONS = 2
GROUPS = 4
EXPERTS = 8
IMG_DEV = 8
IMAGES = 32
ROWS = 394
CAP = 128


def draw_w_qkv(key, part):
    shape = (SECTIONS, 3, D, D)
    return (jax.random.truncated_normal(jax.random.fold_in(key, 21), -4.0, 4.0, shape, jnp.float32) * D ** (-0.5)).astype(jnp.bfloat16)


def draw_w_router(key, part):
    shape = (SECTIONS, D, EXPERTS)
    return jax.random.truncated_normal(jax.random.fold_in(key, 31), -4.0, 4.0, shape, jnp.float32) * (0.3 * D ** (-0.5))


def route_tables(key):
    key = jax.random.fold_in(key, 7)
    blocks = SECTIONS * IMAGES // IMG_MB
    block_rows = IMG_MB * SEQ
    hot = jax.random.randint(jax.random.fold_in(key, 1), (blocks, 1), 0, EXPERTS)
    first = jax.random.randint(jax.random.fold_in(key, 2), (blocks, block_rows), 0, EXPERTS)
    first = jnp.where(jnp.arange(block_rows)[None, :] <= CAP, hot, first)
    second = (first + jax.random.randint(jax.random.fold_in(key, 3), (blocks, block_rows), 1, EXPERTS)) % EXPERTS
    chosen = jnp.concatenate([first, second], axis=1)
    marks = (chosen[:, :, None] == jnp.arange(EXPERTS)[None, None, :]).astype(jnp.int32)
    ranks = jnp.sum((jnp.cumsum(marks, axis=1) - marks) * marks, axis=2)
    ranks = jnp.where(ranks < CAP, ranks, -1)
    shape = (SECTIONS, IMAGES, SEQ, 2)
    route_out = jnp.stack([first, second], axis=-1).reshape(shape).astype(jnp.int32)
    slot_out = jnp.stack([ranks[:, :block_rows], ranks[:, block_rows:]], axis=-1).reshape(shape).astype(jnp.int32)
    return (route_out, slot_out)


def draw_routes(key, part):
    return route_tables(key)[0]


def draw_slots(key, part):
    return route_tables(key)[1]


def levels(key, extent, cuts, smallest, largest):
    def one(dim, parts):
        heights = jax.random.uniform(jax.random.fold_in(jax.random.fold_in(key, 6), dim), (parts,), jnp.float32, smallest / len(cuts), largest / len(cuts))
        return jnp.repeat(jnp.exp(heights), extent[dim] // parts).reshape((-1,) + (1,) * (len(extent) - dim - 1))

    factor_of = one(*cuts[0])
    for cut in cuts[1:]:
        factor_of = factor_of * one(*cut)
    return factor_of


def normal_values(rng, shape, width, limit, cuts=(), held_as=jnp.bfloat16):
    values = jax.random.normal(rng, shape, jnp.float32) * width
    if len(cuts) > 0:
        values = levels(rng, shape, cuts, -0.22, 0.18) * values
    return jnp.clip(values, min=-limit, max=limit).astype(held_as)


def setup_inputs(seed: int = 0) -> dict:
    splits = jax.random.split(jax.random.key(seed), 15)
    return {
        "tokens": normal_values(splits[0], (IMAGES, SEQ, D), 1.0, 6.0, ((0, 4),)),
        "batch_order": jax.vmap(lambda own: jax.random.permutation(own, IMG_DEV))(jax.random.split(splits[1], GROUPS)).reshape((GROUPS, IMG_DEV)).astype(jnp.int32),
        "gain_attn": jnp.clip(1.0 + 0.1 * jax.random.normal(splits[2], (SECTIONS, D), jnp.float32), 0.5, 1.5),
        "shift_attn": normal_values(splits[3], (SECTIONS, D), 0.5, 3.0, ((0, 2),), jnp.float32),
        "w_qkv": draw_w_qkv(jax.random.fold_in(splits[14], 71), 0),
        "w_out": normal_values(splits[5], (SECTIONS, D, D), (D // 16) ** -0.5, 0.875, ((0, 2), (1, 4))),
        "gain_moe": jnp.clip(1.0 + 0.1 * jax.random.normal(splits[6], (SECTIONS, D), jnp.float32), 0.5, 1.5),
        "shift_moe": normal_values(splits[7], (SECTIONS, D), 0.5, 3.0, ((0, 2),), jnp.float32),
        "w_router": draw_w_router(jax.random.fold_in(splits[14], 71), 0),
        "w_in": normal_values(splits[9], (SECTIONS, EXPERTS, D, FF), D ** -0.5, 0.21875, ((0, 2), (1, 4), (3, 4))),
        "w_back": normal_values(splits[10], (SECTIONS, EXPERTS, FF, D), (FF // 16) ** -0.5, 0.4375, ((0, 2), (1, 4), (2, 4))),
        "routes": draw_routes(jax.random.fold_in(splits[14], 71), 0),
        "slots": draw_slots(jax.random.fold_in(splits[14], 71), 0),
        "cotangent": normal_values(splits[13], (IMAGES, SEQ, D), 1.0, 6.0, ((0, 4),)),
    }


NORM_EPS = 1e-06
HIGHEST = lax.Precision.HIGHEST

@jax.custom_vjp
def low(v):
    return lax.optimization_barrier(v.astype(jnp.bfloat16)).astype(jnp.float32)

@jax.custom_vjp
def low_back(v):
    return v

def low_keep(v):
    return (low(v), None)

def low_pass(kept, grad):
    return (grad,)

def back_keep(v):
    return (v, None)

def back_low(kept, grad):
    return (low(grad),)
low.defvjp(low_keep, low_pass)
low_back.defvjp(back_keep, back_low)

def round_both(values):
    return low_back(low(values))

def layer_norm(values, gain, shift):
    centred = values - lax.optimization_barrier(jnp.mean(values, axis=-1, keepdims=True))
    inverse = lax.rsqrt(lax.optimization_barrier(jnp.mean(centred * centred, axis=-1, keepdims=True)) + NORM_EPS)
    return centred * inverse * gain + shift

def attend(projected):
    queries, key_rows, value_rows = projected
    scores = low_back(jnp.einsum('shd,thd->hst', queries, key_rows, precision=HIGHEST) * HEAD ** (-0.5))
    attn_probs = jax.nn.softmax(scores, axis=-1)
    return jnp.einsum('hst,thd->shd', low(attn_probs), value_rows, precision=HIGHEST)

def block_layer(current, weights, route_block, slot_block):
    gain_one, shift_one, wqkv, wout, gain_two, shift_two, wrouter, win, wback = weights
    blocks = current.shape[0]
    normed = low(layer_norm(current, gain_one, shift_one))
    flat_rows = normed.reshape(-1, D)
    images = flat_rows.shape[0] // SEQ
    projected = tuple((round_both(jnp.dot(flat_rows, wqkv[proj_index], precision=HIGHEST)).reshape(images, SEQ, HEADS, HEAD) for proj_index in range(3)))
    mixed_heads = lax.map(jax.checkpoint(attend), projected)
    mixed_heads = round_both(mixed_heads.reshape(-1, D))
    attended = low_back(jnp.dot(mixed_heads, wout, precision=HIGHEST))
    hidden = current + attended.reshape(blocks, ROWS, D)
    normed_m = layer_norm(hidden, gain_two, shift_two)
    router_probs = jax.nn.softmax(jnp.einsum('brd,de->bre', normed_m, wrouter, precision=HIGHEST), axis=-1)
    choose = jax.nn.one_hot(route_block, EXPERTS, dtype=jnp.float32)
    gate_values = jnp.einsum('bre,brke->brk', router_probs, choose, precision=HIGHEST)
    target = jnp.where(slot_block >= 0, route_block * CAP + slot_block, -1)
    tables = jax.nn.one_hot(target, EXPERTS * CAP, dtype=jnp.float32)
    sent_rows = low_back(jnp.einsum('brks,brd->bsd', tables, low(normed_m), precision=HIGHEST)).reshape(blocks, EXPERTS, CAP, D)
    pre_act = low_back(jnp.einsum('becd,edf->becf', sent_rows, win, precision=HIGHEST))
    activated = low(jax.nn.gelu(pre_act, approximate=False))
    expert_out = round_both(jnp.einsum('becf,efd->becd', activated, wback, precision=HIGHEST)).reshape(blocks, EXPERTS * CAP, D)
    selected = jnp.einsum('brks,bsd->brkd', tables, expert_out, precision=HIGHEST)
    return hidden + lax.optimization_barrier(jnp.sum(gate_values[..., None] * selected, axis=2))

def reference(tokens, batch_order, gain_attn, shift_attn, w_qkv, w_out, gain_moe, shift_moe, w_router, w_in, w_back, routes, slots, cotangent):
    offsets = (jnp.arange(GROUPS, dtype=jnp.int32) * IMG_DEV)[:, None]
    picked = (offsets + batch_order).reshape(-1).astype(jnp.int32)
    blocks = GROUPS * MB
    inputs = jnp.take(tokens, picked, axis=0).astype(jnp.float32).reshape(blocks, ROWS, D)
    targets = jnp.take(cotangent, picked, axis=0).astype(jnp.float32).reshape(blocks, ROWS, D)
    route_blocks = routes.reshape(SECTIONS, blocks, ROWS, TOPK)
    slot_blocks = slots.reshape(SECTIONS, blocks, ROWS, TOPK)
    weights = (gain_attn, shift_attn, w_qkv.astype(jnp.float32), w_out.astype(jnp.float32), gain_moe, shift_moe, w_router, w_in.astype(jnp.float32), w_back.astype(jnp.float32))
    section_taps = jnp.zeros((SECTIONS - 1, blocks, ROWS, D), jnp.float32)

    def forward(weights, inputs, section_taps):
        current = inputs
        section_outs = []
        for section_index in range(SECTIONS):
            if section_index > 0:
                current = round_both(current) + section_taps[section_index - 1]
            layer_weights = tuple((weight_item[section_index] for weight_item in weights))
            current = block_layer(current, layer_weights, route_blocks[section_index], slot_blocks[section_index])
            section_outs.append(current)
        return (current, jnp.stack(section_outs))
    final_out, pullback, outs_all = jax.vjp(forward, weights, inputs, section_taps, has_aux=True)
    grad_weights, grad_inputs, grad_taps = pullback(targets)
    section_grads = jnp.concatenate([grad_inputs[None], grad_taps], axis=0)
    acts = jnp.zeros((SECTIONS, IMAGES, SEQ, D), jnp.bfloat16).at[:, picked].set(outs_all.reshape(SECTIONS, IMAGES, SEQ, D).astype(jnp.bfloat16))
    in_grads = jnp.zeros((SECTIONS, IMAGES, SEQ, D), jnp.float32).at[:, picked].set(section_grads.reshape(SECTIONS, IMAGES, SEQ, D))
    return (acts, in_grads, grad_weights[0], grad_weights[1], grad_weights[2], grad_weights[3], grad_weights[4], grad_weights[5], grad_weights[6], grad_weights[7], grad_weights[8])
```

```python
from types import SimpleNamespace

import jax
import jax.numpy as jnp
from jax import lax
from jax.experimental import pallas as pl
from jax.experimental.pallas import tpu as pltpu
from jax.sharding import PartitionSpec as P


HEAD = 64
TOPK = 2
MB = 4
IMG_MB = 2
NORM_EPS = 1e-06
HIGHEST = lax.Precision.HIGHEST
LOW = jnp.bfloat16
F32 = jnp.float32


SECTION, EXPERT, TENSOR = "section", "expert", "tensor"


def swap(value):
    return lax.ppermute(value, SECTION, [(0, 1), (1, 0)])


def across(value, flip):
    count = lax.axis_size(TENSOR)
    return lax.ppermute(value, TENSOR, [(i, i ^ flip) for i in range(count)])


def along(value, flip):
    count = lax.axis_size(EXPERT)
    return lax.ppermute(value, EXPERT, [(i, i ^ flip) for i in range(count)])


def hop(value, flip_expert, flip_tensor):
    owners, count = lax.axis_size(EXPERT), lax.axis_size(TENSOR)
    pairs = [
        (e * count + t, (e ^ flip_expert) * count + (t ^ flip_tensor))
        for e in range(owners)
        for t in range(count)
    ]
    return lax.ppermute(value, (EXPERT, TENSOR), pairs)


def to_sibling(value, layer):
    return lax.ppermute(value, SECTION, [(layer, 1 - layer)])


def to_owner(value, layer):
    return lax.ppermute(value, SECTION, [(1 - layer, layer)])


def V(value):
    return value, pltpu.VMEM


def A(value):
    return value, pl.ANY


def S(value):
    return value, pltpu.SMEM


def O(shape, dtype, count=None, space=pltpu.VMEM):
    return shape, dtype, count, space


def named(names, flat):
    result, place = {}, 0
    for key, count in names:
        if count is None:
            result[key] = flat[place]
            place += 1
        else:
            result[key] = list(flat[place : place + count])
            place += count
    return result


def run(body, ins, outs, scratch=None, flops=0):
    scratch = scratch or {}
    arrays, in_specs, in_names = [], [], []
    for key, (value, space) in ins.items():
        many = isinstance(value, (list, tuple))
        in_names.append((key, len(value) if many else None))
        for item in value if many else [value]:
            arrays.append(item)
            in_specs.append(pl.BlockSpec(memory_space=space))
    shapes, out_specs, out_names = [], [], []
    for key, (shape, dtype, count, space) in outs.items():
        out_names.append((key, count))
        for _ in range(1 if count is None else count):
            shapes.append(jax.ShapeDtypeStruct(shape, dtype))
            out_specs.append(pl.BlockSpec(memory_space=space))
    n_in, n_out = len(arrays), len(shapes)

    def kernel(*refs):
        names = named(in_names, refs[:n_in])
        names.update(named(out_names, refs[n_in : n_in + n_out]))
        names.update(zip(scratch.keys(), refs[n_in + n_out :]))
        body(SimpleNamespace(**names))

    moved = sum(a.size * a.dtype.itemsize for a in arrays)
    moved += sum(s.size * jnp.dtype(s.dtype).itemsize for s in shapes)
    cost = pl.CostEstimate(flops=int(flops), bytes_accessed=int(moved), transcendentals=0)
    results = pl.pallas_call(
        kernel,
        out_shape=tuple(shapes),
        in_specs=in_specs,
        out_specs=tuple(out_specs),
        scratch_shapes=list(scratch.values()),
        cost_estimate=cost,
    )(*arrays)
    return SimpleNamespace(**named(out_names, results))


def dot(left, right, precision=None):
    return jnp.dot(left, right, preferred_element_type=F32, precision=precision)


def dot_nt(left, right, precision=None):
    return lax.dot_general(
        left, right, (((1,), (1,)), ((), ())), preferred_element_type=F32, precision=precision
    )


def dot_tn(left, right, precision=None):
    return lax.dot_general(
        left, right, (((0,), (0,)), ((), ())), preferred_element_type=F32, precision=precision
    )


def unit_rows(values):
    centred = values - jnp.mean(values, axis=-1, keepdims=True)
    inverse = lax.rsqrt(jnp.mean(centred * centred, axis=-1, keepdims=True) + NORM_EPS)
    return centred * inverse, inverse


def norm_back(grad, unit, inverse, gain):
    scaled = grad * gain
    inner = (
        scaled
        - jnp.mean(scaled, axis=-1, keepdims=True)
        - unit * jnp.mean(scaled * unit, axis=-1, keepdims=True)
    )
    return inner * inverse


def gelu_pair(pre_act):
    normal_cdf = 0.5 * (1.0 + lax.erf(pre_act * 0.7071067811865476))
    density = jnp.exp(-0.5 * pre_act * pre_act) * 0.3989422804014327
    return pre_act * normal_cdf, normal_cdf + pre_act * density


def fetch(owner, direct, forwarded, target, sem):
    @pl.when(owner)
    def _():
        pltpu.make_async_copy(direct, target, sem).start()

    @pl.when(jnp.logical_not(owner))
    def _():
        pltpu.make_async_copy(forwarded, target, sem).start()


def arrived(target, sem):
    pltpu.make_async_copy(target, target, sem).wait()


def image_of(ns, flip, other):
    return ns.order[(ns.info[2] ^ flip) * IMG_MB + (ns.info[0] ^ other)]


def lanes(count):
    return lax.broadcasted_iota(jnp.int32, (1, count), 1)


def one_hot(index, count):
    return index == lanes(count)


def plan(cfg, picks, others):
    size = cfg.padded

    def body(ns):
        first, expert, mine = ns.info[0] == 0, ns.info[1], ns.info[3]
        for layer in range(2):
            here = ns.info[0] == layer
            picks = jnp.where(here, ns.picks[...], ns.others[...])
            pairs = []
            for i in range(2):
                part = picks[4 * i : 4 * i + 4, :]
                pairs.append((part[0:TOPK, :], part[TOPK:, :]))
            own = [jnp.where(first, low, high) for low, high in pairs]
            other = [jnp.where(first, high, low) for low, high in pairs]
            for i, (route, slot) in enumerate((own, other)):
                route = jnp.maximum(route, 0)
                chunk = (((route >> 1) ^ expert) << 1) + ((route & 1) ^ mine)
                half = jnp.where(slot >= cfg.rows, 1, 0)
                index = chunk * cfg.rows + slot - half * cfg.rows
                sent = (slot >= 0) & (half == ns.info[0])
                ns.targets[layer][TOPK * i : TOPK * (i + 1), :] = jnp.where(sent, index, -1)
                if i == 0:
                    full = jnp.where(slot >= 0, (half ^ ns.info[0]) * cfg.slots + index, -1)
                    ns.wide[...] = jnp.zeros_like(ns.wide)
                    ns.wide[0:TOPK, 0:size] = route.astype(F32)
                    ns.wide[TOPK : 2 * TOPK, 0:size] = full.astype(F32)
                    tall = ns.wide[...].T
                    ns.columns[layer][...] = tall[0:size, 0 : 2 * TOPK].astype(jnp.int32)

    ins = dict(info=S(cfg.info), picks=V(picks), others=V(others))
    outs = dict(
        targets=O((2 * TOPK, size), jnp.int32, 2), columns=O((size, 2 * TOPK), jnp.int32, 2)
    )
    scratch = dict(wide=pltpu.VMEM((128, (size + 127) // 128 * 128), F32))
    return run(body, ins, outs, scratch)


def combine(ns, cfg):
    gather_rows(cfg, ns.mine, ns.ye)
    gather_rows(cfg, ns.theirs, ns.ye, cfg.slots)
    total = ns.hid_in[...]
    for k in range(TOPK):
        table = one_hot(ns.cols_in[:, 2 + k : 3 + k], 2 * cfg.slots).astype(F32).astype(LOW)
        chosen = dot(table, ns.ye[...])
        ns.sel[k] = chosen.astype(LOW)
        total = total + ns.gates_in[:, k : k + 1] * chosen
    return total


def gather_rows(cfg, chunks, target, base=0):
    for c in range(cfg.chunks):
        target[base + c * cfg.rows : base + (c + 1) * cfg.rows, :] = chunks[c][...]


def fetch_halves(first, direct, forwarded, target, sems):
    half = target.shape[0] // 2
    fetch(first, direct, forwarded, target.at[0:half], sems.at[0])
    fetch(first, forwarded, direct, target.at[half:], sems.at[1])


def wait_halves(target, sems):
    half = target.shape[0] // 2
    arrived(target.at[0:half], sems.at[0])
    arrived(target.at[half:], sems.at[1])


def fetch_attention(ns, cfg):
    first = ns.info[0] == 0
    for d in range(cfg.tensor):
        queries, out = [ns.wq_d[d], ns.wq_f[d]], None
        if not ns.joined:
            out = [ns.wo_d[d], ns.wo_f[d]]
        if ns.joined:
            part = 3 * cfg.cols // 2
            out = [ref.at[part:] for ref in queries]
            queries = [ref.at[0:part] for ref in queries]
        fetch_halves(first, *queries, ns.wq.at[d], ns.sem.at[0, d])
        fetch_halves(first, *out, ns.wo.at[d], ns.sem.at[1, d])


def wait_attention(ns, d):
    wait_halves(ns.wq.at[d], ns.sem.at[0, d])
    wait_halves(ns.wo.at[d], ns.sem.at[1, d])


def project(ns, cfg, d, rows):
    cols = cfg.cols
    return [
        dot_nt(rows, ns.wq[d, i * cols : (i + 1) * cols, :]).astype(LOW) for i in range(3)
    ]


def softmax_rows(scores, real):
    scores = jnp.where(real, scores, -1e30)
    largest = jnp.max(scores, axis=-1, keepdims=True)
    shifted = jnp.exp(scores - largest)
    total = jnp.sum(shifted, axis=-1, keepdims=True)
    return shifted / total, largest + jnp.log(total)


def heads_forward(cfg, queries, keys, values):
    head_of = lanes(cfg.cols) // HEAD
    real = lanes(cfg.padded) < cfg.seq
    zero = jnp.zeros((), LOW)
    mixed = jnp.zeros((cfg.padded, cfg.cols), F32)
    logs = []
    for h in range(cfg.heads):
        scores = dot_nt(jnp.where(head_of == h, queries, zero), keys) * HEAD ** (-0.5)
        probs, log = softmax_rows(scores, real)
        mixed = mixed + dot(probs.astype(LOW), jnp.where(head_of == h, values, zero))
        logs.append(log)
    return mixed.astype(LOW), logs


def normed_rows(ns, rows):
    unit, _ = unit_rows(rows)
    return (unit * ns.pack[0:1, :] + ns.pack[1:2, :]).astype(LOW)


def route_rows(ns, cfg):
    unit, _ = unit_rows(ns.hid[...])
    normed = unit * ns.pack[2:3, :] + ns.pack[3:4, :]
    ns.mm[...] = normed.astype(LOW)
    logits = dot_nt(normed, ns.pack[4 : 4 + cfg.experts, :], HIGHEST)
    logits = logits - jnp.max(logits, axis=-1, keepdims=True)
    probs = jnp.exp(logits)
    probs = probs / jnp.sum(probs, axis=-1, keepdims=True)
    ns.probs[...] = probs
    gates = jnp.zeros((cfg.padded, 128), F32)
    for k in range(TOPK):
        hot = one_hot(ns.cols[:, k : k + 1], cfg.experts)
        gate = jnp.sum(jnp.where(hot, probs, 0.0), axis=-1, keepdims=True)
        gates = jnp.where(lanes(128) == k, gate, gates)
    ns.gates[...] = gates


def route_outs(cfg):
    rows, width = cfg.padded, cfg.width
    return dict(
        hid=O((rows, width), F32),
        mm=O((rows, width), LOW),
        probs=O((rows, cfg.experts), F32),
        gates=O((rows, 128), F32),
    )


def attention_flops(cfg):
    return cfg.padded * cfg.width * cfg.width * 8 + 4 * cfg.padded**2 * cfg.width * 4


def attention_heads(cfg, tokens, direct, forwarded, pack):
    def body(ns):
        fetch(ns.info[0] == 0, ns.direct, ns.forwarded, ns.wq.at[0], ns.sem.at[0])
        for d in range(cfg.tensor):
            ns.z[d][0 : cfg.seq, :] = ns.tokens[image_of(ns, d, 0)]
            ns.z[d][cfg.seq :, :] = jnp.zeros((cfg.padded - cfg.seq, cfg.width), LOW)
            ns.a[d] = normed_rows(ns, ns.z[d][...].astype(F32))
        arrived(ns.wq.at[0], ns.sem.at[0])

        def chunk(d, carry):
            ns.mixed[d] = heads_forward(cfg, *project(ns, cfg, 0, ns.a[d]))[0]
            return carry

        lax.fori_loop(0, cfg.tensor, chunk, 0)
        for d in range(cfg.tensor):
            ns.o[d][...] = ns.mixed[d]

    ins = dict(
        info=S(cfg.info),
        order=S(cfg.order),
        tokens=V(tokens),
        direct=A(direct),
        forwarded=A(forwarded),
        pack=V(pack),
    )
    outs = dict(
        o=O((cfg.padded, cfg.cols), LOW, cfg.tensor), z=O((cfg.padded, cfg.width), LOW, cfg.tensor)
    )
    scratch = dict(
        wq=pltpu.VMEM((1, 3 * cfg.cols, cfg.width), LOW),
        a=pltpu.VMEM((cfg.tensor, cfg.padded, cfg.width), LOW),
        mixed=pltpu.VMEM((cfg.tensor, cfg.padded, cfg.cols), LOW),
        sem=pltpu.SemaphoreType.DMA((1,)),
    )
    return run(body, ins, outs, scratch, attention_flops(cfg))


def attention_out(cfg, rows, mixed, weights, pack, cols):
    def body(ns):
        first = ns.info[0] == 0
        for d in range(cfg.tensor):
            fetch_halves(first, ns.wo_d[d], ns.wo_f[d], ns.wo.at[d], ns.sem.at[d])
        total = ns.z[...].astype(F32)
        for d in range(cfg.tensor):
            wait_halves(ns.wo.at[d], ns.sem.at[d])
            total = total + dot(ns.mixed[d][...], ns.wo[d])
        ns.hid[...] = total
        route_rows(ns, cfg)

    ins = dict(
        info=S(cfg.info),
        z=V(rows),
        mixed=V(mixed),
        wo_d=A(weights.wo_d),
        wo_f=A(weights.wo_f),
        pack=V(pack),
        cols=V(cols),
    )
    scratch = dict(
        wo=pltpu.VMEM((cfg.tensor, cfg.cols, cfg.width), LOW),
        sem=pltpu.SemaphoreType.DMA((cfg.tensor, 2)),
    )
    flops = 2 * cfg.padded * cfg.width * cfg.width
    return run(body, ins, route_outs(cfg), scratch, flops)


def combine_ins(mine, theirs, saved, cols):
    return dict(
        mine=V(mine),
        theirs=V(theirs),
        hid_in=V(saved.hid),
        gates_in=V(saved.gates),
        cols_in=V(cols),
    )


def combine_outs(cfg):
    return dict(
        out=O((cfg.padded, cfg.width), LOW), sel=O((TOPK, cfg.padded, cfg.width), LOW)
    )


def combine_attention(cfg, mine, theirs, saved, cols_in, weights, pack, cols):
    def body(ns):
        ns.joined = True
        fetch_attention(ns, cfg)
        ns.out[...] = combine(ns, cfg).astype(LOW)
        rows = ns.out[...].astype(F32)
        ns.a[...] = normed_rows(ns, rows)
        ns.hid[...] = rows
        ns.lse[...] = jnp.zeros_like(ns.lse)

        def chunk(d, carry):
            wait_attention(ns, d)
            parts = project(ns, cfg, d, ns.a[...])
            for i in range(3):
                ns.qkv[d, i] = parts[i]
            mixed, logs = heads_forward(cfg, *parts)
            for h in range(cfg.heads):
                place = lanes(128) == cfg.heads * d + h
                ns.lse[...] = jnp.where(place, logs[h], ns.lse[...])
            ns.mixed[d] = mixed
            ns.hid[...] += dot(mixed, ns.wo[d])
            return carry

        lax.fori_loop(0, cfg.tensor, chunk, 0)
        for d in range(cfg.tensor):
            ns.o[d][...] = ns.mixed[d]
        route_rows(ns, cfg)

    ins = dict(info=S(cfg.info), pack=V(pack), cols=V(cols))
    ins.update(combine_ins(mine, theirs, saved, cols_in))
    ins.update(weights.attention())
    outs = {**combine_outs(cfg), **route_outs(cfg)}
    outs.update(
        qkv=O((cfg.tensor, 3, cfg.padded, cfg.cols), LOW),
        lse=O((cfg.padded, 128), F32),
        o=O((cfg.padded, cfg.cols), LOW, cfg.tensor),
    )
    scratch = dict(
        wq=pltpu.VMEM((cfg.tensor, 3 * cfg.cols, cfg.width), LOW),
        wo=pltpu.VMEM((cfg.tensor, cfg.cols, cfg.width), LOW),
        a=pltpu.VMEM((cfg.padded, cfg.width), LOW),
        mixed=pltpu.VMEM((cfg.tensor, cfg.padded, cfg.cols), LOW),
        ye=pltpu.VMEM((2 * cfg.slots, cfg.width), LOW),
        sem=pltpu.SemaphoreType.DMA((2, cfg.tensor, 2)),
    )
    return run(body, ins, outs, scratch, attention_flops(cfg))


def last_combine(cfg, mine, theirs, saved, cols_in):
    def body(ns):
        ns.out[...] = combine(ns, cfg).astype(LOW)

    scratch = dict(ye=pltpu.VMEM((2 * cfg.slots, cfg.width), LOW))
    flops = 8 * cfg.padded * cfg.slots * cfg.width
    ins = combine_ins(mine, theirs, saved, cols_in)
    return run(body, ins, combine_outs(cfg), scratch, flops)


def slot_rows(ns, cfg, image, choices):
    place = lax.broadcasted_iota(jnp.int32, (cfg.slots, cfg.padded), 0)
    hot = None
    for k in choices:
        row = TOPK * image + k
        here = place == ns.targets[row : row + 1, :]
        hot = here if hot is None else hot | here
    return hot.astype(F32).astype(LOW)


def send_rows(ns, cfg, rows):
    for c in range(cfg.chunks):
        ns.sent[c][...] = rows[c * cfg.rows : (c + 1) * cfg.rows, :]


def dispatch(cfg, mine, theirs, targets):
    def body(ns):
        rows = dot(slot_rows(ns, cfg, 0, range(TOPK)), ns.mine[...])
        rows = rows + dot(slot_rows(ns, cfg, 1, range(TOPK)), ns.theirs[...])
        send_rows(ns, cfg, rows.astype(LOW))

    ins = dict(mine=V(mine), theirs=V(theirs), targets=V(targets))
    outs = dict(sent=O((cfg.rows, cfg.width), LOW, cfg.chunks))
    return run(body, ins, outs, None, 4 * cfg.slots * cfg.padded * cfg.width).sent


def dispatch_back(cfg, mine, theirs, gates_mine, gates_theirs, targets):
    whole = theirs is None

    def body(ns):
        if whole:
            grads = (ns.rows, ns.other)
            for i, grad in enumerate(grads):
                grad[0 : cfg.seq, :] = ns.mine[image_of(ns, 0, i)]
                grad[cfg.seq :, :] = jnp.zeros((cfg.padded - cfg.seq, cfg.width), LOW)
        else:
            grads = (ns.mine, ns.theirs)
        rows = jnp.zeros((cfg.slots, cfg.width), F32)
        for image, (grad, gates) in enumerate(zip(grads, (ns.gates_mine, ns.gates_theirs))):
            for k in range(TOPK):
                weighted = (gates[:, k : k + 1] * grad[...].astype(F32)).astype(LOW)
                rows = rows + dot(slot_rows(ns, cfg, image, (k,)), weighted)
        send_rows(ns, cfg, rows.astype(LOW))

    ins = dict(
        mine=V(mine),
        gates_mine=V(gates_mine),
        gates_theirs=V(gates_theirs),
        targets=V(targets),
        info=S(cfg.info),
    )
    outs = dict(sent=O((cfg.rows, cfg.width), LOW, cfg.chunks))
    scratch = None
    if whole:
        ins.update(order=S(cfg.order))
        outs.update(rows=O((cfg.padded, cfg.width), LOW))
        scratch = dict(other=pltpu.VMEM((cfg.padded, cfg.width), LOW))
    else:
        ins.update(theirs=V(theirs))
    flops = 8 * cfg.slots * cfg.padded * cfg.width
    return run(body, ins, outs, scratch, flops)


TILE = 256


def fetch_experts(ns, d, matrix):
    first = ns.info[0] == 0
    if matrix == 0:
        fetch(first, ns.we_d[d], ns.we_f[d], ns.wi.at[d], ns.sem.at[0, d])
    else:
        fetch(first, ns.we_f[d], ns.we_d[d], ns.wb.at[d], ns.sem.at[1, d])


def expert_scratch(cfg):
    return dict(
        wi=pltpu.VMEM((cfg.tensor, cfg.width, cfg.hidden), LOW),
        wb=pltpu.VMEM((cfg.tensor, cfg.hidden, cfg.width), LOW),
        acc=pltpu.VMEM((cfg.slots, cfg.width), F32),
        sem=pltpu.SemaphoreType.DMA((3, cfg.tensor)),
        out_sem=pltpu.SemaphoreType.DMA((2, cfg.tensor)),
    )


def expert_flops(cfg):
    return 4 * cfg.slots * cfg.width * cfg.hidden * cfg.tensor


def experts_forward(cfg, chunks, weights):
    def body(ns):
        for d in range(cfg.tensor):
            fetch_experts(ns, d, 0)
            fetch_experts(ns, d, 1)
        gather_rows(cfg, ns.chunks, ns.x)
        ns.acc[...] = jnp.zeros_like(ns.acc)

        def chunk(d, carry):
            arrived(ns.wi.at[d], ns.sem.at[0, d])
            for place in range(0, cfg.slots, TILE):
                part = slice(place, place + TILE)
                act, slope = gelu_pair(dot(ns.x[part, :], ns.wi[d]))
                ns.act_s[d, part, :] = act.astype(LOW)
                ns.slope_s[d, part, :] = slope.astype(LOW)
            arrived(ns.wb.at[d], ns.sem.at[1, d])
            ns.acc[...] += dot(ns.act_s[d], ns.wb[d])
            pltpu.make_async_copy(ns.act_s.at[d], ns.act.at[d], ns.out_sem.at[0, d]).start()
            pltpu.make_async_copy(ns.slope_s.at[d], ns.slope.at[d], ns.out_sem.at[1, d]).start()
            return carry

        lax.fori_loop(0, cfg.tensor, chunk, 0)
        for c in range(cfg.chunks):
            ns.ye[c][...] = ns.acc[c * cfg.rows : (c + 1) * cfg.rows, :].astype(LOW)
        for d in range(cfg.tensor):
            arrived(ns.act_s.at[d], ns.out_sem.at[0, d])
            arrived(ns.slope_s.at[d], ns.out_sem.at[1, d])

    ins = dict(info=S(cfg.info), chunks=V(chunks), **weights.experts())
    hidden = (cfg.tensor, cfg.slots, cfg.hidden)
    outs = dict(
        x=O((cfg.slots, cfg.width), LOW),
        ye=O((cfg.rows, cfg.width), LOW, cfg.chunks),
        act=O(hidden, LOW, space=pl.ANY),
        slope=O(hidden, LOW, space=pl.ANY),
    )
    scratch = dict(
        act_s=pltpu.VMEM(hidden, LOW), slope_s=pltpu.VMEM(hidden, LOW), **expert_scratch(cfg)
    )
    return run(body, ins, outs, scratch, expert_flops(cfg))


def experts_back(cfg, chunks, rows, act, slope, weights):
    def body(ns):
        first = ns.info[0] == 0
        for d in range(cfg.tensor):
            fetch_experts(ns, d, 1)
            pltpu.make_async_copy(ns.slope.at[d], ns.slope_s.at[d], ns.sem.at[2, d]).start()
            fetch_experts(ns, d, 0)

            @pl.when(first)
            def _():
                pltpu.make_async_copy(ns.act.at[d], ns.act_s.at[d], ns.act_sem.at[d]).start()

        gather_rows(cfg, ns.chunks, ns.x)
        ns.acc[...] = jnp.zeros_like(ns.acc)

        def chunk(d, carry):
            arrived(ns.wb.at[d], ns.sem.at[1, d])
            arrived(ns.slope_s.at[d], ns.sem.at[2, d])
            arrived(ns.wi.at[d], ns.sem.at[0, d])
            for place in range(0, cfg.slots, TILE):
                part = slice(place, place + TILE)
                grad = dot_nt(ns.x[part, :], ns.wb[d]) * ns.slope_s[d, part, :].astype(F32)
                grad = grad.astype(LOW)
                ns.dpre_s[d, part, :] = grad
                ns.acc[part, :] += dot_nt(grad, ns.wi[d])
            pltpu.make_async_copy(ns.dpre_s.at[d], ns.dpre.at[d], ns.out_sem.at[0, d]).start()

            @pl.when(first)
            def _():
                arrived(ns.act_s.at[d], ns.act_sem.at[d])

            fetch(first, ns.act_s.at[d], ns.dpre_s.at[d], ns.hidden.at[d], ns.out_sem.at[1, d])
            return carry

        lax.fori_loop(0, cfg.tensor, chunk, 0)
        ns.rows_out[...] = jnp.where(first, ns.x[...].astype(F32), ns.rows[...].astype(F32)).astype(LOW)
        for c in range(cfg.chunks):
            ns.dxe[c][...] = ns.acc[c * cfg.rows : (c + 1) * cfg.rows, :].astype(LOW)
        for d in range(cfg.tensor):
            arrived(ns.dpre_s.at[d], ns.out_sem.at[0, d])
            arrived(ns.dpre_s.at[d], ns.out_sem.at[1, d])

    ins = dict(
        info=S(cfg.info),
        chunks=V(chunks),
        rows=V(rows),
        act=A(act),
        slope=A(slope),
        **weights.experts(),
    )
    hidden = (cfg.tensor, cfg.slots, cfg.hidden)
    outs = dict(
        x=O((cfg.slots, cfg.width), LOW),
        dxe=O((cfg.rows, cfg.width), LOW, cfg.chunks),
        dpre=O(hidden, LOW, space=pl.ANY),
        rows_out=O((cfg.slots, cfg.width), LOW),
        hidden=O(hidden, LOW, space=pl.ANY),
    )
    scratch = dict(
        dpre_s=pltpu.VMEM(hidden, LOW),
        slope_s=pltpu.VMEM(hidden, LOW),
        act_s=pltpu.VMEM(hidden, LOW),
        act_sem=pltpu.SemaphoreType.DMA((cfg.tensor,)),
        **expert_scratch(cfg),
    )
    return run(body, ins, outs, scratch, expert_flops(cfg))


def experts_grads(cfg, xe, dye, act, dpre, rows, hidden):
    size = cfg.slots

    def body(ns):
        first = ns.info[0] == 0
        fetch(first, ns.xe, ns.dye, ns.fixed.at[0:size], ns.fixed_sem.at[0])
        pltpu.make_async_copy(ns.rows, ns.fixed.at[size:], ns.fixed_sem.at[1]).start()
        for d in range(cfg.tensor):
            fetch(first, ns.dpre.at[d], ns.act.at[d], ns.moving.at[d, 0:size], ns.sem.at[0, d])
            pltpu.make_async_copy(
                ns.hidden.at[d], ns.moving.at[d, size:], ns.sem.at[1, d]
            ).start()
        arrived(ns.fixed.at[0:size], ns.fixed_sem.at[0])
        arrived(ns.fixed.at[size:], ns.fixed_sem.at[1])
        ns.turned[...] = ns.fixed[...].T

        def chunk(d, carry):
            arrived(ns.moving.at[d, 0:size], ns.sem.at[0, d])
            arrived(ns.moving.at[d, size:], ns.sem.at[1, d])
            ns.out_s[d] = dot(ns.turned[...], ns.moving[d]).astype(LOW)
            for k in range(cfg.tensor):

                @pl.when(d == k)
                def _():
                    pltpu.make_async_copy(ns.out_s.at[k], ns.out[k], ns.out_sem.at[k]).start()

            return carry

        lax.fori_loop(0, cfg.tensor, chunk, 0)
        for d in range(cfg.tensor):
            arrived(ns.out_s.at[d], ns.out_sem.at[d])

    ins = dict(
        info=S(cfg.info),
        xe=A(xe),
        dye=A(dye),
        act=A(act),
        dpre=A(dpre),
        rows=A(rows),
        hidden=A(hidden),
    )
    shape = (cfg.width, cfg.hidden)
    outs = dict(out=O(shape, LOW, cfg.tensor, space=pl.ANY))
    scratch = dict(
        fixed=pltpu.VMEM((2 * size, cfg.width), LOW),
        turned=pltpu.VMEM((cfg.width, 2 * size), LOW),
        moving=pltpu.VMEM((cfg.tensor, 2 * size, cfg.hidden), LOW),
        out_s=pltpu.VMEM((cfg.tensor,) + shape, LOW),
        fixed_sem=pltpu.SemaphoreType.DMA((2,)),
        sem=pltpu.SemaphoreType.DMA((2, cfg.tensor)),
        out_sem=pltpu.SemaphoreType.DMA((cfg.tensor,)),
    )
    return run(body, ins, outs, scratch, expert_flops(cfg)).out


def back_to_attention(cfg, grad, saved, sel, mine, theirs, pack, cols):
    def body(ns):
        gather_rows(cfg, ns.mine, ns.dx)
        gather_rows(cfg, ns.theirs, ns.dx, cfg.slots)
        grad = ns.grad[...].astype(F32)
        grad_probs = jnp.zeros((cfg.padded, cfg.experts), F32)
        hot = None
        for k in range(TOPK):
            grad_gate = jnp.sum(grad * ns.sel[k].astype(F32), axis=-1, keepdims=True)
            route = one_hot(ns.cols[:, k : k + 1], cfg.experts)
            grad_probs = grad_probs + jnp.where(route, grad_gate, 0.0)
            place = one_hot(ns.cols[:, 2 + k : 3 + k], 2 * cfg.slots)
            hot = place if hot is None else hot | place
        probs = ns.probs[...]
        grad_logits = probs * (
            grad_probs - jnp.sum(probs * grad_probs, axis=-1, keepdims=True)
        )
        grad_norm = dot(hot.astype(F32).astype(LOW), ns.dx[...])
        grad_norm = grad_norm + dot(grad_logits, ns.pack[4 : 4 + cfg.experts, :], HIGHEST)
        unit, inverse = unit_rows(ns.hid[...])
        gain = ns.pack[2:3, :]
        normed = unit * gain + ns.pack[3:4, :]
        e = cfg.experts
        ns.small[...] = jnp.zeros_like(ns.small)
        ns.small[0:e, :] = dot_tn(grad_logits, normed, HIGHEST)
        ns.small[e : e + 1, :] = jnp.sum(grad_norm * unit, axis=0, keepdims=True)
        ns.small[e + 1 : e + 2, :] = jnp.sum(grad_norm, axis=0, keepdims=True)
        grad_hidden = grad + norm_back(grad_norm, unit, inverse, gain)
        ns.dh[...] = grad_hidden
        ns.datt[0 : cfg.padded, :] = grad_hidden.astype(LOW)
        ns.datt[cfg.padded :, :] = ns.small[...].astype(LOW)

    ins = dict(
        grad=V(grad),
        sel=V(sel),
        mine=V(mine),
        theirs=V(theirs),
        hid=V(saved.hid),
        probs=V(saved.probs),
        pack=V(pack),
        cols=V(cols),
    )
    outs = dict(
        dh=O((cfg.padded, cfg.width), F32),
        datt=O((cfg.padded + cfg.small, cfg.width), LOW),
    )
    scratch = dict(
        dx=pltpu.VMEM((2 * cfg.slots, cfg.width), LOW),
        small=pltpu.VMEM((cfg.small, cfg.width), F32),
    )
    flops = 4 * cfg.padded * cfg.slots * cfg.width
    return run(body, ins, outs, scratch, flops)


def attention_back(cfg, rows, saved, back, weights, pack, again):
    def body(ns):
        ns.joined = not again
        fetch_attention(ns, cfg)
        cols = cfg.cols
        head_of = lanes(cols) // HEAD
        real = lanes(cfg.padded) < cfg.seq
        zero = jnp.zeros((), LOW)
        ns.acc[...] = jnp.zeros_like(ns.acc)
        if again:
            ns.a[...] = normed_rows(ns, ns.z[...].astype(F32))

        def chunk(d, carry):
            wait_attention(ns, d)
            grad_mixed = dot_nt(ns.datt[0 : cfg.padded, :], ns.wo[d]).astype(LOW)
            if again:
                queries, keys, values = project(ns, cfg, d, ns.a[...])
            else:
                queries, keys, values = ns.qkv[d, 0], ns.qkv[d, 1], ns.qkv[d, 2]
            grad_q = jnp.zeros((cfg.padded, cols), F32)
            grad_k, grad_v = grad_q, grad_q
            for h in range(cfg.heads):
                mine = head_of == h
                query = jnp.where(mine, queries, zero)
                grad_head = jnp.where(mine, grad_mixed, zero)
                scores = dot_nt(query, keys) * HEAD ** (-0.5)
                if again:
                    probs, _ = softmax_rows(scores, real)
                else:
                    place = lanes(128) == cfg.heads * d + h
                    lse = jnp.sum(jnp.where(place, ns.lse[...], 0.0), axis=-1, keepdims=True)
                    probs = jnp.exp(jnp.where(real, scores - lse, -1e30))
                grad_v = grad_v + dot_tn(probs.astype(LOW), grad_head)
                grad_probs = dot_nt(grad_head, values)
                inner = jnp.sum(probs * grad_probs, axis=-1, keepdims=True)
                grad_scores = (probs * (grad_probs - inner)).astype(LOW)
                grad_q = grad_q + dot(grad_scores, jnp.where(mine, keys, zero))
                grad_k = grad_k + dot_tn(grad_scores, query)
            grads = (grad_q * HEAD ** (-0.5), grad_k * HEAD ** (-0.5), grad_v)
            total = ns.acc[...]
            for i, grad in enumerate(grads):
                grad = grad.astype(LOW)
                ns.grads[d, i] = grad
                total = total + dot(grad, ns.wq[d, i * cols : (i + 1) * cols, :])
            ns.acc[...] = total
            return carry

        lax.fori_loop(0, cfg.tensor, chunk, 0)
        unit, inverse = unit_rows(ns.z[...].astype(F32))
        grad = ns.acc[...]
        dz = (ns.dh[...] + norm_back(grad, unit, inverse, ns.pack[0:1, :])).astype(LOW)
        ns.dz[...] = dz
        ns.small[...] = jnp.zeros_like(ns.small)
        ns.small[0:1, :] = jnp.sum(grad * unit, axis=0, keepdims=True)
        ns.small[1:2, :] = jnp.sum(grad, axis=0, keepdims=True)
        small = ns.small[...].astype(LOW)
        rows = cfg.padded
        for d in range(cfg.tensor):
            for i in range(3):
                ns.sent[d][0:rows, i * cols : (i + 1) * cols] = ns.grads[d, i]
            if again:
                ns.sent[d][rows : rows + 16, :] = small[:, 0 : 3 * cols]
                ns.sent[d][rows + 16 :, 0:cols] = small[:, 3 * cols :]
            else:
                ns.sent[d][:, 3 * cols :] = ns.o[d][...]
        if not again:
            width, end = cfg.width, rows + cfg.small
            ns.common[0:end, 0:width] = ns.datt[...]
            ns.common[end:, 0:width] = small
            ns.common[0:rows, width:] = dz

    ins = dict(
        info=S(cfg.info),
        z=V(rows),
        pack=V(pack),
        datt=V(back.datt),
        dh=V(back.dh),
        **weights.attention(),
    )
    scratch = dict(
        wq=pltpu.VMEM((cfg.tensor, 3 * cfg.cols, cfg.width), LOW),
        wo=pltpu.VMEM((cfg.tensor, cfg.cols, cfg.width), LOW),
        acc=pltpu.VMEM((cfg.padded, cfg.width), F32),
        grads=pltpu.VMEM((cfg.tensor, 3, cfg.padded, cfg.cols), LOW),
        sem=pltpu.SemaphoreType.DMA((2, cfg.tensor, 2)),
    )
    if again:
        scratch.update(a=pltpu.VMEM((cfg.padded, cfg.width), LOW))
    else:
        ins.update(qkv=V(saved.qkv), lse=V(saved.lse), o=V(saved.o))
    scratch.update(small=pltpu.VMEM((16, cfg.width), F32))
    shape = (cfg.padded + 32, 3 * cfg.cols)
    outs = dict(dz=O((cfg.padded, cfg.width), LOW))
    if not again:
        shape = (cfg.padded, cfg.width)
        outs.update(common=O((cfg.padded + cfg.small + 16, 2 * cfg.width), LOW))
    outs.update(sent=O(shape, LOW, cfg.tensor))
    return run(body, ins, outs, scratch, 2 * attention_flops(cfg))


def pair_sum(values):
    while len(values) > 1:
        values = [a + b for a, b in zip(values[::2], values[1::2])]
    return values[0]


def attention_grads(cfg, rows, sent, datt, mixed, pack):
    joined = mixed is None
    cols, width, padded, small = cfg.cols, cfg.width, cfg.padded, cfg.small

    def body(ns):
        first = ns.info[0] == 0
        upper, lower = [], []
        for d in range(cfg.tensor):
            part = slice(d * padded, (d + 1) * padded)
            ns.a[part, :] = normed_rows(ns, ns.rows[d][...].astype(F32))
            ns.g[part, :] = ns.sent[d][0:padded, 0 : 3 * cols]
            ns.t[part, :] = ns.datt[d][0:padded, 0:width]
            upper.append(ns.datt[d][padded : padded + small, 0:width].astype(F32))
            if joined:
                ns.m[part, :] = ns.sent[d][0:padded, 3 * cols : width]
                lower.append(ns.datt[d][padded + small :, 0:width].astype(F32))
            else:
                ns.m[part, :] = ns.mixed[d][...]
                left = ns.sent[d][padded : padded + 16, :].astype(F32)
                right = ns.sent[d][padded + 16 :, 0:cols].astype(F32)
                lower.append(jnp.concatenate([left, right], axis=1))
        ns.acc[0 : 3 * cols, :] = dot_tn(ns.g[...], ns.a[...])
        ns.acc[3 * cols :, :] = dot_tn(ns.m[...], ns.t[...])
        low, high = ns.acc[0 : 2 * cols, :], ns.acc[2 * cols :, :]
        rest = 2 * cols
        ns.keep[0:rest, :] = jnp.where(first, low, high)
        ns.send[0:rest, :] = jnp.where(first, high, low).astype(LOW)
        upper, lower = pair_sum(upper), pair_sum(lower)
        ns.keep[rest : rest + small, :] = upper
        ns.keep[rest + small :, :] = lower
        ns.send[rest : rest + small, :] = upper.astype(LOW)
        ns.send[rest + small :, :] = lower.astype(LOW)

    ins = dict(info=S(cfg.info), rows=V(rows), sent=V(sent), datt=V(datt), pack=V(pack))
    if not joined:
        ins.update(mixed=V(mixed))
    shape = (2 * cols + small + 16, width)
    outs = dict(keep=O(shape, F32), send=O(shape, LOW))
    every = cfg.tensor * padded
    scratch = dict(
        a=pltpu.VMEM((every, width), LOW),
        g=pltpu.VMEM((every, 3 * cols), LOW),
        t=pltpu.VMEM((every, width), LOW),
        m=pltpu.VMEM((every, cols), LOW),
        acc=pltpu.VMEM((4 * cols, width), F32),
    )
    flops = 8 * cfg.tensor * padded * width * cols
    return run(body, ins, outs, scratch, flops)


def split_owners(cfg, keeps, received):
    part, rest = 2 * cfg.cols // cfg.owners, 2 * cfg.cols

    def body(ns):
        for layer in range(2):
            ns.total[...] = ns.keep[layer][...] + ns.received[layer][...].astype(F32)
            for z in range(cfg.owners):
                place = pl.multiple_of((ns.info[1] ^ z) * part, 8)
                ns.pieces[z][layer, 0:part, :] = ns.total[pl.ds(place, part), :].astype(LOW)
                ns.pieces[z][layer, part:, :] = ns.total[rest:, :].astype(LOW)

    ins = dict(info=S(cfg.info), keep=V(keeps), received=V(received))
    outs = dict(pieces=O((2, part + cfg.small + 16, cfg.width), LOW, cfg.owners))
    scratch = dict(total=pltpu.VMEM(keeps[0].shape, F32))
    return run(body, ins, outs, scratch).pieces


def sum_pieces(cfg, pieces):
    part = 2 * cfg.cols // cfg.owners

    def body(ns):
        total = pair_sum([piece[...].astype(F32) for piece in ns.pieces])
        ns.total[...] = total[:, 0:part, :].astype(LOW)
        ns.small[...] = total[:, part:, :]

    outs = dict(
        total=O((2, part, cfg.width), LOW), small=O((2, cfg.small + 16, cfg.width), F32)
    )
    return run(body, dict(pieces=V(pieces)), outs)


def order_attention_grads(cfg, pieces, small):
    part = 2 * cfg.cols // cfg.owners

    def body(ns):
        def place_layer(mine):
            for z in range(cfg.owners):
                place = pl.ds(pl.multiple_of((ns.info[1] ^ z) * part, 8), part)
                ns.own_s[place, :] = ns.pieces[z][mine].astype(F32)
                ns.send_s[place, :] = ns.pieces[z][1 - mine].astype(F32)
            ns.out[...] = ns.small[mine]

        pl.when(ns.info[0] == 0)(lambda: place_layer(0))
        pl.when(ns.info[0] == 1)(lambda: place_layer(1))
        ns.own[...] = ns.own_s[...].astype(LOW)
        ns.send[...] = ns.send_s[...].astype(LOW)

    ins = dict(info=S(cfg.info), pieces=V(pieces), small=V(small))
    shape = (2 * cfg.cols, cfg.width)
    outs = dict(own=O(shape, LOW), send=O(shape, LOW), out=O(small.shape[1:], F32))
    scratch = dict(own_s=pltpu.VMEM(shape, F32), send_s=pltpu.VMEM(shape, F32))
    return run(body, ins, outs, scratch)


def place_attention_grads(cfg, own, received):
    cols = cfg.cols

    def body(ns):
        first = ns.info[0] == 0
        low = jnp.where(first, ns.own[...].astype(F32), ns.received[...].astype(F32))
        high = jnp.where(first, ns.received[...].astype(F32), ns.own[...].astype(F32))
        ns.qkv[0, 0] = low[0:cols, :]
        ns.qkv[0, 1] = low[cols:, :]
        ns.qkv[0, 2] = high[0:cols, :]
        ns.out[0] = high[cols:, :]

    ins = dict(info=S(cfg.info), own=V(own), received=V(received))
    outs = dict(qkv=O((1, 3, cols, cfg.width), F32), out=O((1, cols, cfg.width), F32))
    return run(body, ins, outs)


def place_expert_grads(cfg, mine, theirs):
    def body(ns):
        sources = ((ns.mine0, ns.theirs0), (ns.mine1, ns.theirs1))
        for layer in range(2):

            @pl.when(ns.info[0] == layer)
            def _():
                for i in range(2):
                    for j in range(2):
                        matrix = j if layer == 0 else 1 - j
                        pltpu.make_async_copy(
                            sources[layer][j][i], ns.held.at[matrix, i], ns.sem.at[matrix, i]
                        ).start()

        for i in range(2):
            expert = ns.info[3] ^ i
            arrived(ns.held.at[0, i], ns.sem.at[0, i])
            ns.grad_in[0, expert] = ns.held[0, i].astype(F32)
            arrived(ns.held.at[1, i], ns.sem.at[1, i])
            ns.grad_back[0, expert] = ns.held[1, i].T.astype(F32)

    ins = dict(
        info=S(cfg.info),
        mine0=A(mine[0]),
        mine1=A(mine[1]),
        theirs0=A(theirs[0]),
        theirs1=A(theirs[1]),
    )
    outs = dict(
        grad_in=O((1, 2, cfg.width, cfg.hidden), F32),
        grad_back=O((1, 2, cfg.hidden, cfg.width), F32),
    )
    scratch = dict(
        held=pltpu.VMEM((2, 2, cfg.width, cfg.hidden), LOW),
        sem=pltpu.SemaphoreType.DMA((2, 2)),
    )
    return run(body, ins, outs, scratch)


def stack_images(values, place):
    low, high, left, right = place

    def body(ns):
        for d, value in enumerate(ns.values):
            ns.out[d] = value[low:high, left:right]

    outs = dict(out=O((len(values), high - low, right - left), LOW))
    return run(body, dict(values=V(values)), outs).out


def place_images(cfg, mine, theirs, lefts, dtype):
    def body(ns):
        def place_layer(own, other, left):
            for d in range(cfg.tensor):
                image = own[d][0 : cfg.seq, left : left + cfg.width]
                ns.images[0, image_of(ns, d, 0)] = image.astype(dtype)
                ns.images[0, image_of(ns, d, 1)] = other[d, 0 : cfg.seq, :].astype(dtype)

        pl.when(ns.info[0] == 0)(lambda: place_layer(ns.mine0, ns.theirs0, lefts[0]))
        pl.when(ns.info[0] == 1)(lambda: place_layer(ns.mine1, ns.theirs1, lefts[1]))

    ins = dict(
        info=S(cfg.info),
        order=S(cfg.order),
        mine0=V(mine[0]),
        mine1=V(mine[1]),
        theirs0=V(theirs[0]),
        theirs1=V(theirs[1]),
    )
    outs = dict(images=O((1, 2 * cfg.tensor, cfg.seq, cfg.width), dtype))
    return run(body, ins, outs).images


def exchange(cfg, chunks):
    return [
        value if c == 0 else hop(value, *divmod(c, cfg.local))
        for c, value in enumerate(chunks)
    ]


def swaps(chunks):
    return [swap(v) for v in chunks]


def forward_chunks(chunks):
    return swaps(chunks[:3]) + swaps(chunks[3:])


def gather_images(value):
    return [value] + [across(value, d) for d in (1, 2, 3)]


def relay_images(value):
    two = across(value, 2)
    one = across(value, 1)
    three = across(two, 1)
    return [value, one, two, three]


def spread(chunks):
    return [chunks[0]] + [across(chunks[d], d) for d in range(1, len(chunks))]


def relay(own, other):
    one = across(other, 1)
    two = across(own, 2)
    three = across(one, 2)
    return [own, one, two, three]


class Weights:
    wo_d = None

    def attention(self):
        parts = dict(wq_d=A(self.wq_d), wq_f=A(self.wq_f))
        if self.wo_d is not None:
            parts.update(wo_d=A(self.wo_d), wo_f=A(self.wo_f))
        return parts

    def experts(self):
        return dict(we_d=A(self.we_d), we_f=A(self.we_f))


def add(left, right):
    return (left.astype(F32) + right.astype(F32)).astype(LOW)


def program(
    tokens,
    batch_order,
    gain_attn,
    shift_attn,
    w_qkv,
    w_out,
    gain_moe,
    shift_moe,
    w_router,
    w_in,
    w_back,
    routes,
    slots,
    cotangent,
):
    section, expert, tensor = (lax.axis_index(n) for n in (SECTION, EXPERT, TENSOR))
    owners, count = lax.axis_size(EXPERT), lax.axis_size(TENSOR)
    local = w_in.shape[1]
    seq, width = tokens.shape[1], tokens.shape[2]
    experts = local * owners
    capacity = (TOPK * IMG_MB * seq * 5 // (4 * experts) + 7) // 8 * 8
    padded = (seq + 15) // 16 * 16
    small = (experts + 2 + 15) // 16 * 16
    cfg = SimpleNamespace(
        tensor=count,
        owners=owners,
        local=local,
        experts=experts,
        seq=seq,
        width=width,
        padded=padded,
        small=small,
        cols=w_qkv.shape[3],
        heads=w_qkv.shape[3] // HEAD,
        hidden=w_in.shape[3],
        chunks=owners * local,
        rows=capacity // 2,
        slots=owners * local * capacity // 2,
    )
    assert count == MB == 4 and local == 2 and IMG_MB == 2 and cfg.width == cfg.hidden
    local_expert = tensor % local
    cfg.info = jnp.stack([section, expert, tensor, local_expert]).astype(jnp.int32)
    cfg.order = batch_order[0]
    first_core = section == 0
    wq = w_qkv[0].transpose(0, 2, 1).reshape(3 * cfg.cols, width)
    wo = w_out[0]
    wq_half, wo_half = 3 * cfg.cols // 2, cfg.cols // 2
    sibling_wq = to_sibling(wq, 0)
    pack = jnp.concatenate([gain_attn, shift_attn, gain_moe, shift_moe, w_router[0].T], axis=0)
    other_pack = swap(pack)
    packs = [
        jnp.where(first_core, pack, other_pack),
        jnp.where(first_core, other_pack, pack),
    ]
    picks = jnp.stack(
        [v[0].reshape(MB, IMG_MB, seq, TOPK)[tensor] for v in (routes, slots)]
    ).transpose(0, 1, 3, 2)
    picks = jnp.pad(picks, ((0, 0), (0, 0), (0, 0), (0, padded - seq)), constant_values=-1)
    picks = picks.reshape(4 * TOPK, padded)
    planned = plan(cfg, picks, swap(picks))
    targets, columns = planned.targets, planned.columns

    def pick(values, index):
        return lax.dynamic_index_in_dim(values, index, 0, keepdims=False)

    weights = [Weights(), Weights()]
    sibling_wo = to_sibling(wo[wo_half:], 0)
    sibling_we = to_sibling(w_back[0], 0)
    wo_own = jnp.where(first_core, wo[:wo_half], sibling_wo)
    weights[0].wo_d = gather_images(wo_own)
    weights[0].wo_f = swaps(weights[0].wo_d)

    def pair(lower, upper):
        return [
            jnp.where(first_core, pick(lower, index), pick(upper, index))
            for index in (local_expert, 1 - local_expert)
        ]

    first_pair = pair(w_in[0], sibling_we)
    weights[0].we_d = relay(*first_pair)
    weights[0].we_f = forward_chunks(weights[0].we_d)
    joined = [jnp.concatenate([wq[:wq_half], wo[:wo_half]], axis=0)]
    joined.append(jnp.concatenate([wq[wq_half:], wo[wo_half:]], axis=0))
    joined = jnp.where(first_core, to_owner(joined[0], 0), joined[1])
    weights[1].wq_d = relay(joined, joined)
    weights[1].wq_f = swaps(weights[1].wq_d)
    sibling_we = to_owner(w_in[0], 0)
    weights[1].we_d = relay(*pair(sibling_we, w_back[0]))
    weights[1].we_f = forward_chunks(weights[1].we_d)
    wq0_own = jnp.where(first_core, wq[:wq_half], sibling_wq[wq_half:])
    weights[0].wq_d = gather_images(wq0_own)
    weights[0].wq_f = swaps(weights[0].wq_d)

    tokens = lax.optimization_barrier((tokens, *first_pair))[0]
    heads = attention_heads(cfg, tokens, wq, sibling_wq, packs[0])
    rows, saved, arrived_rows, forward = [heads.z], [], [], []
    first = attention_out(cfg, heads.z[0], spread(heads.o), weights[0], packs[0], columns[0])
    saved.append(first)
    sent = dispatch(cfg, first.mm, swap(first.mm), targets[0])
    arrived_rows.append(exchange(cfg, sent))
    other_gates = [swap(first.gates)]
    forward.append(experts_forward(cfg, arrived_rows[0], weights[0]))
    mine = exchange(cfg, forward[0].ye)
    second = combine_attention(
        cfg, mine, swaps(mine), first, columns[0], weights[1], packs[1], columns[1]
    )
    saved.append(second)
    other_gates.append(swap(second.gates))
    rows.append(gather_images(second.out))
    sent = dispatch(cfg, second.mm, swap(second.mm), targets[1])
    arrived_rows.append(exchange(cfg, sent))
    sent = dispatch_back(cfg, cotangent, None, second.gates, other_gates[1], targets[1])
    target_rows = sent.rows
    arrived_grads = [None, exchange(cfg, sent.sent)]
    forward.append(experts_forward(cfg, arrived_rows[1], weights[1]))
    mine = exchange(cfg, forward[1].ye)
    final = last_combine(cfg, mine, swaps(mine), second, columns[1])
    last_rows = relay_images(final.out)
    selected = [second.sel, final.sel]

    grad_rows = [None, None, target_rows]
    expert_grads, parts = [None, None], [None, None]
    for layer in (1, 0):
        if layer == 0:
            sent = dispatch_back(
                cfg, grad_rows[1], swap(grad_rows[1]), first.gates, other_gates[0], targets[0]
            )
            arrived_grads[0] = exchange(cfg, sent.sent)
        back = experts_back(
            cfg,
            arrived_grads[layer],
            forward[layer].x,
            forward[layer].act,
            forward[layer].slope,
            weights[layer],
        )
        mine = exchange(cfg, back.dxe)
        zero, one, two, three = experts_grads(
            cfg,
            forward[layer].x,
            back.x,
            forward[layer].act,
            back.dpre,
            swap(back.rows_out),
            swap(back.hidden),
        )
        three = across(three, 2)
        two = across(two, 2)
        one = add(one, three)
        one = across(one, 1)
        own = add(zero, two)
        expert_grads[layer] = (
            [own, one],
            [to_owner(own, layer), to_owner(one, layer)],
        )
        upper = back_to_attention(
            cfg,
            grad_rows[layer + 1],
            saved[layer],
            selected[layer],
            mine,
            swaps(mine),
            packs[layer],
            columns[layer],
        )
        datt = gather_images(upper.datt) if layer == 0 else None
        lower = attention_back(
            cfg, rows[layer][0], saved[layer], upper, weights[layer], packs[layer], layer == 0
        )
        grad_rows[layer] = lower.dz
        sent = spread(lower.sent)
        if layer == 1:
            datt = last_common = relay_images(lower.common)
        grads = attention_grads(
            cfg, rows[layer], sent, datt, heads.o if layer == 0 else None, packs[layer]
        )
        parts[layer] = grads.keep, swap(grads.send)

    split = split_owners(cfg, *zip(*parts))
    split = [split[0]] + [along(split[z], z) for z in range(1, owners)]
    piece = sum_pieces(cfg, split)
    pieces = [piece.total] + [along(piece.total, z) for z in range(1, owners)]

    image = (0, padded, 0, width)
    stacks = [
        to_owner(stack_images(rows[1], image), 0), to_owner(stack_images(last_rows, image), 1)
    ]
    acts = place_images(cfg, [rows[1], last_rows], stacks, (0, 0), LOW)
    first_grads = relay_images(grad_rows[0])
    stacks = [
        to_owner(stack_images(first_grads, image), 0),
        to_owner(stack_images(last_common, (0, padded, width, 2 * width)), 1),
    ]
    in_grads = place_images(cfg, [first_grads, last_common], stacks, (0, width), LOW).astype(F32)
    ordered = order_attention_grads(cfg, pieces, piece.small)
    attention_final = place_attention_grads(cfg, ordered.own, swap(ordered.send))
    final_small = ordered.out
    expert_final = place_expert_grads(cfg, *zip(*expert_grads))
    return (
        acts,
        in_grads,
        final_small[small][None],
        final_small[small + 1][None],
        attention_final.qkv.transpose(0, 1, 3, 2),
        attention_final.out,
        final_small[experts][None],
        final_small[experts + 1][None],
        final_small[:experts].T[None],
        expert_final.grad_in,
        expert_final.grad_back,
    )


def solution(mesh):
    layered = P(SECTION, None)
    attention = P(SECTION, None, None, TENSOR)
    out = P(SECTION, TENSOR, None)
    experts_in = P(SECTION, EXPERT, None, TENSOR)
    experts_back = P(SECTION, EXPERT, TENSOR, None)
    images = P(SECTION, EXPERT, None, None)
    router = P(SECTION, None, None)
    return jax.shard_map(
        program,
        mesh=mesh,
        in_specs=(
            P(EXPERT, None, None),
            P(EXPERT, None),
            layered,
            layered,
            attention,
            out,
            layered,
            layered,
            router,
            experts_in,
            experts_back,
            images,
            images,
            P(EXPERT, None, None),
        ),
        out_specs=(
            images,
            images,
            layered,
            layered,
            attention,
            out,
            layered,
            layered,
            router,
            experts_in,
            experts_back,
        ),
        check_vma=False,
    )
```

```python
from types import SimpleNamespace

import jax
import jax.numpy as jnp
from jax import lax
from jax.experimental import pallas as pl
from jax.experimental.pallas import tpu as pltpu
from jax.sharding import PartitionSpec as P


HEAD = 64
TOPK = 2
MB = 4
IMG_MB = 2
NORM_EPS = 1e-06
HIGHEST = lax.Precision.HIGHEST
LOW = jnp.bfloat16
F32 = jnp.float32


SECTION, EXPERT, TENSOR = "section", "expert", "tensor"


def swap(value):
    return lax.ppermute(value, SECTION, [(0, 1), (1, 0)])


def across(value, flip):
    count = lax.axis_size(TENSOR)
    return lax.ppermute(value, TENSOR, [(i, i ^ flip) for i in range(count)])


def along(value, flip):
    count = lax.axis_size(EXPERT)
    return lax.ppermute(value, EXPERT, [(i, i ^ flip) for i in range(count)])


def hop(value, flip_expert, flip_tensor):
    owners, count = lax.axis_size(EXPERT), lax.axis_size(TENSOR)
    pairs = [
        (e * count + t, (e ^ flip_expert) * count + (t ^ flip_tensor))
        for e in range(owners)
        for t in range(count)
    ]
    return lax.ppermute(value, (EXPERT, TENSOR), pairs)


def V(value):
    return value, pltpu.VMEM


def A(value):
    return value, pl.ANY


def S(value):
    return value, pltpu.SMEM


def O(shape, dtype, count=None, space=pltpu.VMEM):
    return shape, dtype, count, space


def named(names, flat):
    result, place = {}, 0
    for key, count in names:
        if count is None:
            result[key] = flat[place]
            place += 1
        else:
            result[key] = list(flat[place : place + count])
            place += count
    return result


def run(body, ins, outs, scratch=None, flops=0):
    scratch = scratch or {}
    arrays, in_specs, in_names = [], [], []
    for key, (value, space) in ins.items():
        many = isinstance(value, (list, tuple))
        in_names.append((key, len(value) if many else None))
        for item in value if many else [value]:
            arrays.append(item)
            in_specs.append(pl.BlockSpec(memory_space=space))
    shapes, out_specs, out_names = [], [], []
    for key, (shape, dtype, count, space) in outs.items():
        out_names.append((key, count))
        for _ in range(1 if count is None else count):
            shapes.append(jax.ShapeDtypeStruct(shape, dtype))
            out_specs.append(pl.BlockSpec(memory_space=space))
    n_in, n_out = len(arrays), len(shapes)

    def kernel(*refs):
        names = named(in_names, refs[:n_in])
        names.update(named(out_names, refs[n_in : n_in + n_out]))
        names.update(zip(scratch.keys(), refs[n_in + n_out :]))
        body(SimpleNamespace(**names))

    moved = sum(a.size * a.dtype.itemsize for a in arrays)
    moved += sum(s.size * jnp.dtype(s.dtype).itemsize for s in shapes)
    cost = pl.CostEstimate(flops=int(flops), bytes_accessed=int(moved), transcendentals=0)
    results = pl.pallas_call(
        kernel,
        out_shape=tuple(shapes),
        in_specs=in_specs,
        out_specs=tuple(out_specs),
        scratch_shapes=list(scratch.values()),
        cost_estimate=cost,
    )(*arrays)
    return SimpleNamespace(**named(out_names, results))


def dot(left, right, precision=None):
    return jnp.dot(left, right, preferred_element_type=F32, precision=precision)


def dot_nt(left, right, precision=None):
    return lax.dot_general(
        left, right, (((1,), (1,)), ((), ())), preferred_element_type=F32, precision=precision
    )


def dot_tn(left, right, precision=None):
    return lax.dot_general(
        left, right, (((0,), (0,)), ((), ())), preferred_element_type=F32, precision=precision
    )


def unit_rows(values):
    centred = values - jnp.mean(values, axis=-1, keepdims=True)
    inverse = lax.rsqrt(jnp.mean(centred * centred, axis=-1, keepdims=True) + NORM_EPS)
    return centred * inverse, inverse


def norm_back(grad, unit, inverse, gain):
    scaled = grad * gain
    inner = (
        scaled
        - jnp.mean(scaled, axis=-1, keepdims=True)
        - unit * jnp.mean(scaled * unit, axis=-1, keepdims=True)
    )
    return inner * inverse


def gelu_pair(pre_act):
    normal_cdf = 0.5 * (1.0 + lax.erf(pre_act * 0.7071067811865476))
    density = jnp.exp(-0.5 * pre_act * pre_act) * 0.3989422804014327
    return pre_act * normal_cdf, normal_cdf + pre_act * density


def fetch(owner, direct, forwarded, target, sem):
    @pl.when(owner)
    def _():
        pltpu.make_async_copy(direct, target, sem).start()

    @pl.when(jnp.logical_not(owner))
    def _():
        pltpu.make_async_copy(forwarded, target, sem).start()


def arrived(target, sem):
    pltpu.make_async_copy(target, target, sem).wait()


def image_of(ns, flip, other):
    return ns.order[(ns.info[2] ^ flip) * IMG_MB + (ns.info[0] ^ other)]


def lanes(count):
    return lax.broadcasted_iota(jnp.int32, (1, count), 1)


def one_hot(index, count):
    return index == lanes(count)


def plan(cfg, picks, others):
    size = cfg.padded

    def body(ns):
        first, expert, mine = ns.info[0] == 0, ns.info[1], ns.info[3]
        for layer in range(2):
            here = ns.info[0] == layer
            picks = jnp.where(here, ns.picks[...], ns.others[...])
            pairs = []
            for i in range(2):
                part = picks[4 * i : 4 * i + 4, :]
                pairs.append((part[0:TOPK, :], part[TOPK:, :]))
            own = [jnp.where(first, low, high) for low, high in pairs]
            other = [jnp.where(first, high, low) for low, high in pairs]
            for i, (route, slot) in enumerate((own, other)):
                route = jnp.maximum(route, 0)
                chunk = (((route >> 1) ^ expert) << 1) + ((route & 1) ^ mine)
                half = jnp.where(slot >= cfg.rows, 1, 0)
                index = chunk * cfg.rows + slot - half * cfg.rows
                sent = (slot >= 0) & (half == ns.info[0])
                ns.targets[layer][TOPK * i : TOPK * (i + 1), :] = jnp.where(sent, index, -1)
                if i == 0:
                    full = jnp.where(slot >= 0, (half ^ ns.info[0]) * cfg.slots + index, -1)
                    ns.wide[...] = jnp.zeros_like(ns.wide)
                    ns.wide[0:TOPK, 0:size] = route.astype(F32)
                    ns.wide[TOPK : 2 * TOPK, 0:size] = full.astype(F32)
                    tall = ns.wide[...].T
                    ns.columns[layer][...] = tall[0:size, 0 : 2 * TOPK].astype(jnp.int32)

    ins = dict(info=S(cfg.info), picks=V(picks), others=V(others))
    outs = dict(
        targets=O((2 * TOPK, size), jnp.int32, 2), columns=O((size, 2 * TOPK), jnp.int32, 2)
    )
    scratch = dict(wide=pltpu.VMEM((128, (size + 127) // 128 * 128), F32))
    return run(body, ins, outs, scratch)


def combine(ns, cfg):
    gather_rows(cfg, ns.mine, ns.ye)
    gather_rows(cfg, ns.theirs, ns.ye, cfg.slots)
    total = ns.hid_in[...]
    for k in range(TOPK):
        table = one_hot(ns.cols_in[:, 2 + k : 3 + k], 2 * cfg.slots).astype(F32).astype(LOW)
        chosen = dot(table, ns.ye[...])
        ns.sel[k] = chosen.astype(LOW)
        total = total + ns.gates_in[:, k : k + 1] * chosen
    return total


def gather_rows(cfg, chunks, target, base=0):
    for c in range(cfg.chunks):
        target[base + c * cfg.rows : base + (c + 1) * cfg.rows, :] = chunks[c][...]


def fetch_halves(first, direct, forwarded, target, sems):
    half = target.shape[0] // 2
    fetch(first, direct, forwarded, target.at[0:half], sems.at[0])
    fetch(first, forwarded, direct, target.at[half:], sems.at[1])


def wait_halves(target, sems):
    half = target.shape[0] // 2
    arrived(target.at[0:half], sems.at[0])
    arrived(target.at[half:], sems.at[1])


def fetch_attention(ns, cfg):
    first = ns.info[0] == 0
    for d in range(cfg.tensor):
        queries, out = [ns.wq_d[d], ns.wq_f[d]], None
        if not ns.joined:
            out = [ns.wo_d[d], ns.wo_f[d]]
        if ns.joined:
            part = 3 * cfg.cols // 2
            out = [ref.at[part:] for ref in queries]
            queries = [ref.at[0:part] for ref in queries]
        fetch_halves(first, *queries, ns.wq.at[d], ns.sem.at[0, d])
        fetch_halves(first, *out, ns.wo.at[d], ns.sem.at[1, d])


def wait_attention(ns, d):
    wait_halves(ns.wq.at[d], ns.sem.at[0, d])
    wait_halves(ns.wo.at[d], ns.sem.at[1, d])


def project(ns, cfg, d, rows):
    cols = cfg.cols
    return [
        dot_nt(rows, ns.wq[d, i * cols : (i + 1) * cols, :]).astype(LOW) for i in range(3)
    ]


def softmax_rows(scores, real):
    scores = jnp.where(real, scores, -1e30)
    largest = jnp.max(scores, axis=-1, keepdims=True)
    shifted = jnp.exp(scores - largest)
    total = jnp.sum(shifted, axis=-1, keepdims=True)
    return shifted / total, largest + jnp.log(total)


def heads_forward(cfg, queries, keys, values):
    head_of = lanes(cfg.cols) // HEAD
    real = lanes(cfg.padded) < cfg.seq
    zero = jnp.zeros((), LOW)
    mixed = jnp.zeros((cfg.padded, cfg.cols), F32)
    logs = []
    for h in range(cfg.heads):
        scores = dot_nt(jnp.where(head_of == h, queries, zero), keys) * HEAD ** (-0.5)
        probs, log = softmax_rows(scores, real)
        mixed = mixed + dot(probs.astype(LOW), jnp.where(head_of == h, values, zero))
        logs.append(log)
    return mixed.astype(LOW), logs


def normed_rows(ns, rows):
    unit, _ = unit_rows(rows)
    return (unit * ns.pack[0:1, :] + ns.pack[1:2, :]).astype(LOW)


def route_rows(ns, cfg):
    unit, _ = unit_rows(ns.hid[...])
    normed = unit * ns.pack[2:3, :] + ns.pack[3:4, :]
    ns.mm[...] = normed.astype(LOW)
    logits = dot_nt(normed, ns.pack[4 : 4 + cfg.experts, :], HIGHEST)
    logits = logits - jnp.max(logits, axis=-1, keepdims=True)
    probs = jnp.exp(logits)
    probs = probs / jnp.sum(probs, axis=-1, keepdims=True)
    ns.probs[...] = probs
    gates = jnp.zeros((cfg.padded, 128), F32)
    for k in range(TOPK):
        hot = one_hot(ns.cols[:, k : k + 1], cfg.experts)
        gate = jnp.sum(jnp.where(hot, probs, 0.0), axis=-1, keepdims=True)
        gates = jnp.where(lanes(128) == k, gate, gates)
    ns.gates[...] = gates


def route_outs(cfg):
    rows, width = cfg.padded, cfg.width
    return dict(
        hid=O((rows, width), F32),
        mm=O((rows, width), LOW),
        probs=O((rows, cfg.experts), F32),
        gates=O((rows, 128), F32),
    )


def attention_flops(cfg):
    return cfg.padded * cfg.width * cfg.width * 8 + 4 * cfg.padded**2 * cfg.width * 4


def attention_heads(cfg, tokens, direct, forwarded, pack):
    def body(ns):
        fetch(ns.info[0] == 0, ns.direct, ns.forwarded, ns.wq.at[0], ns.sem.at[0])
        for d in range(cfg.tensor):
            ns.z[d][0 : cfg.seq, :] = ns.tokens[image_of(ns, d, 0)]
            ns.z[d][cfg.seq :, :] = jnp.zeros((cfg.padded - cfg.seq, cfg.width), LOW)
            ns.a[d] = normed_rows(ns, ns.z[d][...].astype(F32))
        arrived(ns.wq.at[0], ns.sem.at[0])

        def chunk(d, carry):
            ns.mixed[d] = heads_forward(cfg, *project(ns, cfg, 0, ns.a[d]))[0]
            return carry

        lax.fori_loop(0, cfg.tensor, chunk, 0)
        for d in range(cfg.tensor):
            ns.o[d][...] = ns.mixed[d]

    ins = dict(
        info=S(cfg.info),
        order=S(cfg.order),
        tokens=V(tokens),
        direct=A(direct),
        forwarded=A(forwarded),
        pack=V(pack),
    )
    outs = dict(
        o=O((cfg.padded, cfg.cols), LOW, cfg.tensor), z=O((cfg.padded, cfg.width), LOW, cfg.tensor)
    )
    scratch = dict(
        wq=pltpu.VMEM((1, 3 * cfg.cols, cfg.width), LOW),
        a=pltpu.VMEM((cfg.tensor, cfg.padded, cfg.width), LOW),
        mixed=pltpu.VMEM((cfg.tensor, cfg.padded, cfg.cols), LOW),
        sem=pltpu.SemaphoreType.DMA((1,)),
    )
    return run(body, ins, outs, scratch, attention_flops(cfg))


def attention_out(cfg, rows, mixed, weights, pack, cols):
    def body(ns):
        first = ns.info[0] == 0
        for d in range(cfg.tensor):
            fetch_halves(first, ns.wo_d[d], ns.wo_f[d], ns.wo.at[d], ns.sem.at[d])
        total = ns.z[...].astype(F32)
        for d in range(cfg.tensor):
            wait_halves(ns.wo.at[d], ns.sem.at[d])
            total = total + dot(ns.mixed[d][...], ns.wo[d])
        ns.hid[...] = total
        route_rows(ns, cfg)

    ins = dict(
        info=S(cfg.info),
        z=V(rows),
        mixed=V(mixed),
        wo_d=A(weights.wo_d),
        wo_f=A(weights.wo_f),
        pack=V(pack),
        cols=V(cols),
    )
    scratch = dict(
        wo=pltpu.VMEM((cfg.tensor, cfg.cols, cfg.width), LOW),
        sem=pltpu.SemaphoreType.DMA((cfg.tensor, 2)),
    )
    flops = 2 * cfg.padded * cfg.width * cfg.width
    return run(body, ins, route_outs(cfg), scratch, flops)


def combine_ins(mine, theirs, saved, cols):
    return dict(
        mine=V(mine),
        theirs=V(theirs),
        hid_in=V(saved.hid),
        gates_in=V(saved.gates),
        cols_in=V(cols),
    )


def combine_outs(cfg):
    return dict(
        out=O((cfg.padded, cfg.width), LOW), sel=O((TOPK, cfg.padded, cfg.width), LOW)
    )


def combine_attention(cfg, mine, theirs, saved, cols_in, weights, pack, cols):
    def body(ns):
        ns.joined = True
        fetch_attention(ns, cfg)
        ns.out[...] = combine(ns, cfg).astype(LOW)
        rows = ns.out[...].astype(F32)
        ns.a[...] = normed_rows(ns, rows)
        ns.hid[...] = rows
        ns.lse[...] = jnp.zeros_like(ns.lse)

        def chunk(d, carry):
            wait_attention(ns, d)
            parts = project(ns, cfg, d, ns.a[...])
            for i in range(3):
                ns.qkv[d, i] = parts[i]
            mixed, logs = heads_forward(cfg, *parts)
            for h in range(cfg.heads):
                place = lanes(128) == cfg.heads * d + h
                ns.lse[...] = jnp.where(place, logs[h], ns.lse[...])
            ns.mixed[d] = mixed
            ns.hid[...] += dot(mixed, ns.wo[d])
            return carry

        lax.fori_loop(0, cfg.tensor, chunk, 0)
        for d in range(cfg.tensor):
            ns.o[d][...] = ns.mixed[d]
        route_rows(ns, cfg)

    ins = dict(info=S(cfg.info), pack=V(pack), cols=V(cols))
    ins.update(combine_ins(mine, theirs, saved, cols_in))
    ins.update(weights.attention())
    outs = {**combine_outs(cfg), **route_outs(cfg)}
    outs.update(
        qkv=O((cfg.tensor, 3, cfg.padded, cfg.cols), LOW),
        lse=O((cfg.padded, 128), F32),
        o=O((cfg.padded, cfg.cols), LOW, cfg.tensor),
    )
    scratch = dict(
        wq=pltpu.VMEM((cfg.tensor, 3 * cfg.cols, cfg.width), LOW),
        wo=pltpu.VMEM((cfg.tensor, cfg.cols, cfg.width), LOW),
        a=pltpu.VMEM((cfg.padded, cfg.width), LOW),
        mixed=pltpu.VMEM((cfg.tensor, cfg.padded, cfg.cols), LOW),
        ye=pltpu.VMEM((2 * cfg.slots, cfg.width), LOW),
        sem=pltpu.SemaphoreType.DMA((2, cfg.tensor, 2)),
    )
    return run(body, ins, outs, scratch, attention_flops(cfg))


def last_combine(cfg, mine, theirs, saved, cols_in):
    def body(ns):
        ns.out[...] = combine(ns, cfg).astype(LOW)

    scratch = dict(ye=pltpu.VMEM((2 * cfg.slots, cfg.width), LOW))
    flops = 8 * cfg.padded * cfg.slots * cfg.width
    ins = combine_ins(mine, theirs, saved, cols_in)
    return run(body, ins, combine_outs(cfg), scratch, flops)


def slot_rows(ns, cfg, image, choices):
    place = lax.broadcasted_iota(jnp.int32, (cfg.slots, cfg.padded), 0)
    hot = None
    for k in choices:
        row = TOPK * image + k
        here = place == ns.targets[row : row + 1, :]
        hot = here if hot is None else hot | here
    return hot.astype(F32).astype(LOW)


def send_rows(ns, cfg, rows):
    for c in range(cfg.chunks):
        ns.sent[c][...] = rows[c * cfg.rows : (c + 1) * cfg.rows, :]


def dispatch(cfg, mine, theirs, targets):
    def body(ns):
        rows = dot(slot_rows(ns, cfg, 0, range(TOPK)), ns.mine[...])
        rows = rows + dot(slot_rows(ns, cfg, 1, range(TOPK)), ns.theirs[...])
        send_rows(ns, cfg, rows.astype(LOW))

    ins = dict(mine=V(mine), theirs=V(theirs), targets=V(targets))
    outs = dict(sent=O((cfg.rows, cfg.width), LOW, cfg.chunks))
    return run(body, ins, outs, None, 4 * cfg.slots * cfg.padded * cfg.width).sent


def dispatch_back(cfg, mine, theirs, gates_mine, gates_theirs, targets):
    whole = theirs is None

    def body(ns):
        if whole:
            grads = (ns.rows, ns.other)
            for i, grad in enumerate(grads):
                grad[0 : cfg.seq, :] = ns.mine[image_of(ns, 0, i)]
                grad[cfg.seq :, :] = jnp.zeros((cfg.padded - cfg.seq, cfg.width), LOW)
        else:
            grads = (ns.mine, ns.theirs)
        rows = jnp.zeros((cfg.slots, cfg.width), F32)
        for image, (grad, gates) in enumerate(zip(grads, (ns.gates_mine, ns.gates_theirs))):
            for k in range(TOPK):
                weighted = (gates[:, k : k + 1] * grad[...].astype(F32)).astype(LOW)
                rows = rows + dot(slot_rows(ns, cfg, image, (k,)), weighted)
        send_rows(ns, cfg, rows.astype(LOW))

    ins = dict(
        mine=V(mine),
        gates_mine=V(gates_mine),
        gates_theirs=V(gates_theirs),
        targets=V(targets),
        info=S(cfg.info),
    )
    outs = dict(sent=O((cfg.rows, cfg.width), LOW, cfg.chunks))
    scratch = None
    if whole:
        ins.update(order=S(cfg.order))
        outs.update(rows=O((cfg.padded, cfg.width), LOW))
        scratch = dict(other=pltpu.VMEM((cfg.padded, cfg.width), LOW))
    else:
        ins.update(theirs=V(theirs))
    flops = 8 * cfg.slots * cfg.padded * cfg.width
    return run(body, ins, outs, scratch, flops)


TILE = 256


def fetch_experts(ns, d, matrix):
    first = ns.info[0] == 0
    if matrix == 0:
        fetch(first, ns.we_d[d], ns.we_f[d], ns.wi.at[d], ns.sem.at[0, d])
    else:
        fetch(first, ns.we_f[d], ns.we_d[d], ns.wb.at[d], ns.sem.at[1, d])


def expert_scratch(cfg):
    return dict(
        wi=pltpu.VMEM((cfg.tensor, cfg.width, cfg.hidden), LOW),
        wb=pltpu.VMEM((cfg.tensor, cfg.hidden, cfg.width), LOW),
        acc=pltpu.VMEM((cfg.slots, cfg.width), F32),
        sem=pltpu.SemaphoreType.DMA((3, cfg.tensor)),
        out_sem=pltpu.SemaphoreType.DMA((2, cfg.tensor)),
    )


def expert_flops(cfg):
    return 4 * cfg.slots * cfg.width * cfg.hidden * cfg.tensor


def experts_forward(cfg, chunks, weights):
    def body(ns):
        for d in range(cfg.tensor):
            fetch_experts(ns, d, 0)
            fetch_experts(ns, d, 1)
        gather_rows(cfg, ns.chunks, ns.x)
        ns.acc[...] = jnp.zeros_like(ns.acc)

        def chunk(d, carry):
            arrived(ns.wi.at[d], ns.sem.at[0, d])
            for place in range(0, cfg.slots, TILE):
                part = slice(place, place + TILE)
                act, slope = gelu_pair(dot(ns.x[part, :], ns.wi[d]))
                ns.act_s[d, part, :] = act.astype(LOW)
                ns.slope_s[d, part, :] = slope.astype(LOW)
            arrived(ns.wb.at[d], ns.sem.at[1, d])
            ns.acc[...] += dot(ns.act_s[d], ns.wb[d])
            pltpu.make_async_copy(ns.act_s.at[d], ns.act.at[d], ns.out_sem.at[0, d]).start()
            pltpu.make_async_copy(ns.slope_s.at[d], ns.slope.at[d], ns.out_sem.at[1, d]).start()
            return carry

        lax.fori_loop(0, cfg.tensor, chunk, 0)
        for c in range(cfg.chunks):
            ns.ye[c][...] = ns.acc[c * cfg.rows : (c + 1) * cfg.rows, :].astype(LOW)
        for d in range(cfg.tensor):
            arrived(ns.act_s.at[d], ns.out_sem.at[0, d])
            arrived(ns.slope_s.at[d], ns.out_sem.at[1, d])

    ins = dict(info=S(cfg.info), chunks=V(chunks), **weights.experts())
    hidden = (cfg.tensor, cfg.slots, cfg.hidden)
    outs = dict(
        x=O((cfg.slots, cfg.width), LOW),
        ye=O((cfg.rows, cfg.width), LOW, cfg.chunks),
        act=O(hidden, LOW, space=pl.ANY),
        slope=O(hidden, LOW, space=pl.ANY),
    )
    scratch = dict(
        act_s=pltpu.VMEM(hidden, LOW), slope_s=pltpu.VMEM(hidden, LOW), **expert_scratch(cfg)
    )
    return run(body, ins, outs, scratch, expert_flops(cfg))


def experts_back(cfg, chunks, rows, act, slope, weights):
    def body(ns):
        first = ns.info[0] == 0
        for d in range(cfg.tensor):
            fetch_experts(ns, d, 1)
            pltpu.make_async_copy(ns.slope.at[d], ns.slope_s.at[d], ns.sem.at[2, d]).start()
            fetch_experts(ns, d, 0)

            @pl.when(first)
            def _():
                pltpu.make_async_copy(ns.act.at[d], ns.act_s.at[d], ns.act_sem.at[d]).start()

        gather_rows(cfg, ns.chunks, ns.x)
        ns.acc[...] = jnp.zeros_like(ns.acc)

        def chunk(d, carry):
            arrived(ns.wb.at[d], ns.sem.at[1, d])
            arrived(ns.slope_s.at[d], ns.sem.at[2, d])
            arrived(ns.wi.at[d], ns.sem.at[0, d])
            for place in range(0, cfg.slots, TILE):
                part = slice(place, place + TILE)
                grad = dot_nt(ns.x[part, :], ns.wb[d]) * ns.slope_s[d, part, :].astype(F32)
                grad = grad.astype(LOW)
                ns.dpre_s[d, part, :] = grad
                ns.acc[part, :] += dot_nt(grad, ns.wi[d])
            pltpu.make_async_copy(ns.dpre_s.at[d], ns.dpre.at[d], ns.out_sem.at[0, d]).start()

            @pl.when(first)
            def _():
                arrived(ns.act_s.at[d], ns.act_sem.at[d])

            fetch(first, ns.act_s.at[d], ns.dpre_s.at[d], ns.hidden.at[d], ns.out_sem.at[1, d])
            return carry

        lax.fori_loop(0, cfg.tensor, chunk, 0)
        ns.rows_out[...] = jnp.where(first, ns.x[...].astype(F32), ns.rows[...].astype(F32)).astype(LOW)
        for c in range(cfg.chunks):
            ns.dxe[c][...] = ns.acc[c * cfg.rows : (c + 1) * cfg.rows, :].astype(LOW)
        for d in range(cfg.tensor):
            arrived(ns.dpre_s.at[d], ns.out_sem.at[0, d])
            arrived(ns.dpre_s.at[d], ns.out_sem.at[1, d])

    ins = dict(
        info=S(cfg.info),
        chunks=V(chunks),
        rows=V(rows),
        act=A(act),
        slope=A(slope),
        **weights.experts(),
    )
    hidden = (cfg.tensor, cfg.slots, cfg.hidden)
    outs = dict(
        x=O((cfg.slots, cfg.width), LOW),
        dxe=O((cfg.rows, cfg.width), LOW, cfg.chunks),
        dpre=O(hidden, LOW, space=pl.ANY),
        rows_out=O((cfg.slots, cfg.width), LOW),
        hidden=O(hidden, LOW, space=pl.ANY),
    )
    scratch = dict(
        dpre_s=pltpu.VMEM(hidden, LOW),
        slope_s=pltpu.VMEM(hidden, LOW),
        act_s=pltpu.VMEM(hidden, LOW),
        act_sem=pltpu.SemaphoreType.DMA((cfg.tensor,)),
        **expert_scratch(cfg),
    )
    return run(body, ins, outs, scratch, expert_flops(cfg))


def experts_grads(cfg, xe, dye, act, dpre, rows, hidden):
    size = cfg.slots

    def body(ns):
        first = ns.info[0] == 0
        fetch(first, ns.xe, ns.dye, ns.fixed.at[0:size], ns.fixed_sem.at[0])
        pltpu.make_async_copy(ns.rows, ns.fixed.at[size:], ns.fixed_sem.at[1]).start()
        for d in range(cfg.tensor):
            fetch(first, ns.dpre.at[d], ns.act.at[d], ns.moving.at[d, 0:size], ns.sem.at[0, d])
            pltpu.make_async_copy(
                ns.hidden.at[d], ns.moving.at[d, size:], ns.sem.at[1, d]
            ).start()
        arrived(ns.fixed.at[0:size], ns.fixed_sem.at[0])
        arrived(ns.fixed.at[size:], ns.fixed_sem.at[1])

        def chunk(d, carry):
            arrived(ns.moving.at[d, 0:size], ns.sem.at[0, d])
            arrived(ns.moving.at[d, size:], ns.sem.at[1, d])
            ns.out_s[d] = dot_tn(ns.fixed[...], ns.moving[d]).astype(LOW)
            for k in range(cfg.tensor):

                @pl.when(d == k)
                def _():
                    pltpu.make_async_copy(ns.out_s.at[k], ns.out[k], ns.out_sem.at[k]).start()

            return carry

        lax.fori_loop(0, cfg.tensor, chunk, 0)
        for d in range(cfg.tensor):
            arrived(ns.out_s.at[d], ns.out_sem.at[d])

    ins = dict(
        info=S(cfg.info),
        xe=A(xe),
        dye=A(dye),
        act=A(act),
        dpre=A(dpre),
        rows=A(rows),
        hidden=A(hidden),
    )
    shape = (cfg.width, cfg.hidden)
    outs = dict(out=O(shape, LOW, cfg.tensor, space=pl.ANY))
    scratch = dict(
        fixed=pltpu.VMEM((2 * size, cfg.width), LOW),
        moving=pltpu.VMEM((cfg.tensor, 2 * size, cfg.hidden), LOW),
        out_s=pltpu.VMEM((cfg.tensor,) + shape, LOW),
        fixed_sem=pltpu.SemaphoreType.DMA((2,)),
        sem=pltpu.SemaphoreType.DMA((2, cfg.tensor)),
        out_sem=pltpu.SemaphoreType.DMA((cfg.tensor,)),
    )
    return run(body, ins, outs, scratch, expert_flops(cfg)).out


def back_to_attention(cfg, grad, saved, sel, mine, theirs, pack, cols):
    def body(ns):
        gather_rows(cfg, ns.mine, ns.dx)
        gather_rows(cfg, ns.theirs, ns.dx, cfg.slots)
        grad = ns.grad[...].astype(F32)
        grad_probs = jnp.zeros((cfg.padded, cfg.experts), F32)
        hot = None
        for k in range(TOPK):
            grad_gate = jnp.sum(grad * ns.sel[k].astype(F32), axis=-1, keepdims=True)
            route = one_hot(ns.cols[:, k : k + 1], cfg.experts)
            grad_probs = grad_probs + jnp.where(route, grad_gate, 0.0)
            place = one_hot(ns.cols[:, 2 + k : 3 + k], 2 * cfg.slots)
            hot = place if hot is None else hot | place
        probs = ns.probs[...]
        grad_logits = probs * (
            grad_probs - jnp.sum(probs * grad_probs, axis=-1, keepdims=True)
        )
        grad_norm = dot(hot.astype(F32).astype(LOW), ns.dx[...])
        grad_norm = grad_norm + dot(grad_logits, ns.pack[4 : 4 + cfg.experts, :], HIGHEST)
        unit, inverse = unit_rows(ns.hid[...])
        gain = ns.pack[2:3, :]
        normed = unit * gain + ns.pack[3:4, :]
        e = cfg.experts
        ns.small[...] = jnp.zeros_like(ns.small)
        ns.small[0:e, :] = dot_tn(grad_logits, normed, HIGHEST)
        ns.small[e : e + 1, :] = jnp.sum(grad_norm * unit, axis=0, keepdims=True)
        ns.small[e + 1 : e + 2, :] = jnp.sum(grad_norm, axis=0, keepdims=True)
        grad_hidden = grad + norm_back(grad_norm, unit, inverse, gain)
        ns.dh[...] = grad_hidden
        ns.datt[0 : cfg.padded, :] = grad_hidden.astype(LOW)
        ns.datt[cfg.padded :, :] = ns.small[...].astype(LOW)

    ins = dict(
        grad=V(grad),
        sel=V(sel),
        mine=V(mine),
        theirs=V(theirs),
        hid=V(saved.hid),
        probs=V(saved.probs),
        pack=V(pack),
        cols=V(cols),
    )
    outs = dict(
        dh=O((cfg.padded, cfg.width), F32),
        datt=O((cfg.padded + cfg.small, cfg.width), LOW),
    )
    scratch = dict(
        dx=pltpu.VMEM((2 * cfg.slots, cfg.width), LOW),
        small=pltpu.VMEM((cfg.small, cfg.width), F32),
    )
    flops = 4 * cfg.padded * cfg.slots * cfg.width
    return run(body, ins, outs, scratch, flops)


def attention_back(cfg, rows, saved, back, weights, pack, again):
    def body(ns):
        ns.joined = not again
        fetch_attention(ns, cfg)
        cols = cfg.cols
        head_of = lanes(cols) // HEAD
        real = lanes(cfg.padded) < cfg.seq
        zero = jnp.zeros((), LOW)
        ns.acc[...] = jnp.zeros_like(ns.acc)
        if again:
            ns.a[...] = normed_rows(ns, ns.z[...].astype(F32))

        def chunk(d, carry):
            wait_attention(ns, d)
            grad_mixed = dot_nt(ns.datt[0 : cfg.padded, :], ns.wo[d]).astype(LOW)
            if again:
                queries, keys, values = project(ns, cfg, d, ns.a[...])
            else:
                queries, keys, values = ns.qkv[d, 0], ns.qkv[d, 1], ns.qkv[d, 2]
            grad_q = jnp.zeros((cfg.padded, cols), F32)
            grad_k, grad_v = grad_q, grad_q
            for h in range(cfg.heads):
                mine = head_of == h
                query = jnp.where(mine, queries, zero)
                grad_head = jnp.where(mine, grad_mixed, zero)
                scores = dot_nt(query, keys) * HEAD ** (-0.5)
                if again:
                    probs, _ = softmax_rows(scores, real)
                else:
                    place = lanes(128) == cfg.heads * d + h
                    lse = jnp.sum(jnp.where(place, ns.lse[...], 0.0), axis=-1, keepdims=True)
                    probs = jnp.exp(jnp.where(real, scores - lse, -1e30))
                grad_v = grad_v + dot_tn(probs.astype(LOW), grad_head)
                grad_probs = dot_nt(grad_head, values)
                inner = jnp.sum(probs * grad_probs, axis=-1, keepdims=True)
                grad_scores = (probs * (grad_probs - inner)).astype(LOW)
                grad_q = grad_q + dot(grad_scores, jnp.where(mine, keys, zero))
                grad_k = grad_k + dot_tn(grad_scores, query)
            grads = (grad_q * HEAD ** (-0.5), grad_k * HEAD ** (-0.5), grad_v)
            total = ns.acc[...]
            for i, grad in enumerate(grads):
                grad = grad.astype(LOW)
                ns.grads[d, i] = grad
                total = total + dot(grad, ns.wq[d, i * cols : (i + 1) * cols, :])
            ns.acc[...] = total
            return carry

        lax.fori_loop(0, cfg.tensor, chunk, 0)
        unit, inverse = unit_rows(ns.z[...].astype(F32))
        grad = ns.acc[...]
        dz = (ns.dh[...] + norm_back(grad, unit, inverse, ns.pack[0:1, :])).astype(LOW)
        ns.dz[...] = dz
        ns.small[...] = jnp.zeros_like(ns.small)
        ns.small[0:1, :] = jnp.sum(grad * unit, axis=0, keepdims=True)
        ns.small[1:2, :] = jnp.sum(grad, axis=0, keepdims=True)
        small = ns.small[...].astype(LOW)
        rows = cfg.padded
        for d in range(cfg.tensor):
            for i in range(3):
                ns.sent[d][0:rows, i * cols : (i + 1) * cols] = ns.grads[d, i]
            if again:
                ns.sent[d][rows : rows + 16, :] = small[:, 0 : 3 * cols]
                ns.sent[d][rows + 16 :, 0:cols] = small[:, 3 * cols :]
            else:
                ns.sent[d][:, 3 * cols :] = ns.o[d][...]
        if not again:
            width, end = cfg.width, rows + cfg.small
            ns.common[0:end, 0:width] = ns.datt[...]
            ns.common[end:, 0:width] = small
            ns.common[0:rows, width:] = dz

    ins = dict(
        info=S(cfg.info),
        z=V(rows),
        pack=V(pack),
        datt=V(back.datt),
        dh=V(back.dh),
        **weights.attention(),
    )
    scratch = dict(
        wq=pltpu.VMEM((cfg.tensor, 3 * cfg.cols, cfg.width), LOW),
        wo=pltpu.VMEM((cfg.tensor, cfg.cols, cfg.width), LOW),
        acc=pltpu.VMEM((cfg.padded, cfg.width), F32),
        grads=pltpu.VMEM((cfg.tensor, 3, cfg.padded, cfg.cols), LOW),
        sem=pltpu.SemaphoreType.DMA((2, cfg.tensor, 2)),
    )
    if again:
        scratch.update(a=pltpu.VMEM((cfg.padded, cfg.width), LOW))
    else:
        ins.update(qkv=V(saved.qkv), lse=V(saved.lse), o=V(saved.o))
    scratch.update(small=pltpu.VMEM((16, cfg.width), F32))
    shape = (cfg.padded + 32, 3 * cfg.cols)
    outs = dict(dz=O((cfg.padded, cfg.width), LOW))
    if not again:
        shape = (cfg.padded, cfg.width)
        outs.update(common=O((cfg.padded + cfg.small + 16, 2 * cfg.width), LOW))
    outs.update(sent=O(shape, LOW, cfg.tensor))
    return run(body, ins, outs, scratch, 2 * attention_flops(cfg))


def pair_sum(values):
    while len(values) > 1:
        values = [a + b for a, b in zip(values[::2], values[1::2])]
    return values[0]


def attention_grads(cfg, rows, sent, datt, mixed, pack):
    joined = mixed is None
    cols, width, padded, small = cfg.cols, cfg.width, cfg.padded, cfg.small

    def body(ns):
        first = ns.info[0] == 0
        upper, lower = [], []
        for d in range(cfg.tensor):
            part = slice(d * padded, (d + 1) * padded)
            ns.a[part, :] = normed_rows(ns, ns.rows[d][...].astype(F32))
            ns.g[part, :] = ns.sent[d][0:padded, 0 : 3 * cols]
            ns.t[part, :] = ns.datt[d][0:padded, 0:width]
            upper.append(ns.datt[d][padded : padded + small, 0:width].astype(F32))
            if joined:
                ns.m[part, :] = ns.sent[d][0:padded, 3 * cols : width]
                lower.append(ns.datt[d][padded + small :, 0:width].astype(F32))
            else:
                ns.m[part, :] = ns.mixed[d][...]
                left = ns.sent[d][padded : padded + 16, :].astype(F32)
                right = ns.sent[d][padded + 16 :, 0:cols].astype(F32)
                lower.append(jnp.concatenate([left, right], axis=1))
        ns.acc[0 : 3 * cols, :] = dot_tn(ns.g[...], ns.a[...])
        ns.acc[3 * cols :, :] = dot_tn(ns.m[...], ns.t[...])
        low, high = ns.acc[0 : 2 * cols, :], ns.acc[2 * cols :, :]
        rest = 2 * cols
        ns.keep[0:rest, :] = jnp.where(first, low, high)
        ns.send[0:rest, :] = jnp.where(first, high, low).astype(LOW)
        upper, lower = pair_sum(upper), pair_sum(lower)
        place = cfg.experts + 2
        ns.keep[rest:, :] = upper
        ns.keep[rest + place : rest + place + 2, :] = lower[0:2, :]
        ns.send[rest:, :] = ns.keep[rest:, :].astype(LOW)

    ins = dict(info=S(cfg.info), rows=V(rows), sent=V(sent), datt=V(datt), pack=V(pack))
    if not joined:
        ins.update(mixed=V(mixed))
    shape = (2 * cols + small, width)
    outs = dict(keep=O(shape, F32), send=O(shape, LOW))
    every = cfg.tensor * padded
    scratch = dict(
        a=pltpu.VMEM((every, width), LOW),
        g=pltpu.VMEM((every, 3 * cols), LOW),
        t=pltpu.VMEM((every, width), LOW),
        m=pltpu.VMEM((every, cols), LOW),
        acc=pltpu.VMEM((4 * cols, width), F32),
    )
    flops = 8 * cfg.tensor * padded * width * cols
    return run(body, ins, outs, scratch, flops)


def split_owners(cfg, keeps, received):
    part, rest = 2 * cfg.cols // cfg.owners, 2 * cfg.cols

    def body(ns):
        for layer in range(2):
            ns.total[...] = ns.keep[layer][...] + ns.received[layer][...].astype(F32)
            for z in range(cfg.owners):
                place = pl.multiple_of((ns.info[1] ^ z) * part, 8)
                ns.pieces[z][layer, 0:part, :] = ns.total[pl.ds(place, part), :].astype(LOW)
                ns.pieces[z][layer, part:, :] = ns.total[rest:, :].astype(LOW)

    ins = dict(info=S(cfg.info), keep=V(keeps), received=V(received))
    outs = dict(pieces=O((2, part + cfg.small, cfg.width), LOW, cfg.owners))
    scratch = dict(total=pltpu.VMEM(keeps[0].shape, F32))
    return run(body, ins, outs, scratch).pieces


def sum_pieces(cfg, pieces):
    part = 2 * cfg.cols // cfg.owners

    def body(ns):
        total = pair_sum([piece[...].astype(F32) for piece in ns.pieces])
        ns.total[...] = total[:, 0:part, :].astype(LOW)
        ns.small[...] = total[:, part:, :]

    outs = dict(
        total=O((2, part, cfg.width), LOW), small=O((2, cfg.small, cfg.width), F32)
    )
    return run(body, dict(pieces=V(pieces)), outs)


def order_attention_grads(cfg, pieces, small):
    part = 2 * cfg.cols // cfg.owners

    def body(ns):
        def place_layer(mine):
            for z in range(cfg.owners):
                place = pl.ds(pl.multiple_of((ns.info[1] ^ z) * part, 8), part)
                ns.own_s[place, :] = ns.pieces[z][mine].astype(F32)
                ns.send_s[place, :] = ns.pieces[z][1 - mine].astype(F32)
            ns.out[...] = ns.small[mine]

        pl.when(ns.info[0] == 0)(lambda: place_layer(0))
        pl.when(ns.info[0] == 1)(lambda: place_layer(1))
        ns.own[...] = ns.own_s[...].astype(LOW)
        ns.send[...] = ns.send_s[...].astype(LOW)

    ins = dict(info=S(cfg.info), pieces=V(pieces), small=V(small))
    shape = (2 * cfg.cols, cfg.width)
    outs = dict(own=O(shape, LOW), send=O(shape, LOW), out=O(small.shape[1:], F32))
    scratch = dict(own_s=pltpu.VMEM(shape, F32), send_s=pltpu.VMEM(shape, F32))
    return run(body, ins, outs, scratch)


def place_attention_grads(cfg, own, received):
    cols = cfg.cols

    def body(ns):
        first = ns.info[0] == 0
        low = jnp.where(first, ns.own[...].astype(F32), ns.received[...].astype(F32))
        high = jnp.where(first, ns.received[...].astype(F32), ns.own[...].astype(F32))
        ns.qkv[0, 0] = low[0:cols, :]
        ns.qkv[0, 1] = low[cols:, :]
        ns.qkv[0, 2] = high[0:cols, :]
        ns.out[0] = high[cols:, :]

    ins = dict(info=S(cfg.info), own=V(own), received=V(received))
    outs = dict(qkv=O((1, 3, cols, cfg.width), F32), out=O((1, cols, cfg.width), F32))
    return run(body, ins, outs)


def place_expert_grads(cfg, mine, theirs):
    def body(ns):
        sources = ((ns.mine0, ns.theirs0), (ns.mine1, ns.theirs1))
        for layer in range(2):

            @pl.when(ns.info[0] == layer)
            def _():
                for i in range(2):
                    for j in range(2):
                        matrix = j if layer == 0 else 1 - j
                        pltpu.make_async_copy(
                            sources[layer][j][i], ns.held.at[matrix, i], ns.sem.at[matrix, i]
                        ).start()

        for i in range(2):
            expert = ns.info[3] ^ i
            arrived(ns.held.at[0, i], ns.sem.at[0, i])
            ns.grad_in[0, expert] = ns.held[0, i].astype(F32)
            arrived(ns.held.at[1, i], ns.sem.at[1, i])
            ns.grad_back[0, expert] = ns.held[1, i].T.astype(F32)

    ins = dict(
        info=S(cfg.info),
        mine0=A(mine[0]),
        mine1=A(mine[1]),
        theirs0=A(theirs[0]),
        theirs1=A(theirs[1]),
    )
    outs = dict(
        grad_in=O((1, 2, cfg.width, cfg.hidden), F32),
        grad_back=O((1, 2, cfg.hidden, cfg.width), F32),
    )
    scratch = dict(
        held=pltpu.VMEM((2, 2, cfg.width, cfg.hidden), LOW),
        sem=pltpu.SemaphoreType.DMA((2, 2)),
    )
    return run(body, ins, outs, scratch)


def place_images(cfg, mine, theirs, lefts, dtype):
    def body(ns):
        def place_layer(own, other, left):
            for d in range(cfg.tensor):
                image = own[d][0 : cfg.seq, left : left + cfg.width]
                ns.images[0, image_of(ns, d, 0)] = image.astype(dtype)
                image = other[d][0 : cfg.seq, left : left + cfg.width]
                ns.images[0, image_of(ns, d, 1)] = image.astype(dtype)

        pl.when(ns.info[0] == 0)(lambda: place_layer(ns.mine0, ns.theirs0, lefts[0]))
        pl.when(ns.info[0] == 1)(lambda: place_layer(ns.mine1, ns.theirs1, lefts[1]))

    ins = dict(
        info=S(cfg.info),
        order=S(cfg.order),
        mine0=V(mine[0]),
        mine1=V(mine[1]),
        theirs0=V(theirs[0]),
        theirs1=V(theirs[1]),
    )
    outs = dict(images=O((1, 2 * cfg.tensor, cfg.seq, cfg.width), dtype))
    return run(body, ins, outs).images


def exchange(cfg, chunks):
    return [
        value if c == 0 else hop(value, *divmod(c, cfg.local))
        for c, value in enumerate(chunks)
    ]


def swaps(chunks):
    return [swap(v) for v in chunks]


def forward_chunks(chunks):
    return swaps(chunks[:3]) + swaps(chunks[3:])


def gather_images(value):
    return [value] + [across(value, d) for d in (1, 2, 3)]


def relay_images(value):
    two = across(value, 2)
    one = across(value, 1)
    three = across(two, 1)
    return [value, one, two, three]


def spread(chunks):
    return [chunks[0]] + [across(chunks[d], d) for d in range(1, len(chunks))]


def relay(own, other):
    one = across(other, 1)
    two = across(own, 2)
    three = across(one, 2)
    return [own, one, two, three]


class Weights:
    wo_d = None

    def attention(self):
        parts = dict(wq_d=A(self.wq_d), wq_f=A(self.wq_f))
        if self.wo_d is not None:
            parts.update(wo_d=A(self.wo_d), wo_f=A(self.wo_f))
        return parts

    def experts(self):
        return dict(we_d=A(self.we_d), we_f=A(self.we_f))


def add(left, right):
    return (left.astype(F32) + right.astype(F32)).astype(LOW)


def program(
    tokens,
    batch_order,
    gain_attn,
    shift_attn,
    w_qkv,
    w_out,
    gain_moe,
    shift_moe,
    w_router,
    w_in,
    w_back,
    routes,
    slots,
    cotangent,
):
    section, expert, tensor = (lax.axis_index(n) for n in (SECTION, EXPERT, TENSOR))
    owners, count = lax.axis_size(EXPERT), lax.axis_size(TENSOR)
    local = w_in.shape[1]
    seq, width = tokens.shape[1], tokens.shape[2]
    experts = local * owners
    capacity = (TOPK * IMG_MB * seq * 5 // (4 * experts) + 7) // 8 * 8
    padded = (seq + 15) // 16 * 16
    small = (experts + 4 + 15) // 16 * 16
    cfg = SimpleNamespace(
        tensor=count,
        owners=owners,
        local=local,
        experts=experts,
        seq=seq,
        width=width,
        padded=padded,
        small=small,
        cols=w_qkv.shape[3],
        heads=w_qkv.shape[3] // HEAD,
        hidden=w_in.shape[3],
        chunks=owners * local,
        rows=capacity // 2,
        slots=owners * local * capacity // 2,
    )
    assert count == MB == 4 and local == 2 and IMG_MB == 2 and cfg.width == cfg.hidden
    local_expert = tensor % local
    cfg.info = jnp.stack([section, expert, tensor, local_expert]).astype(jnp.int32)
    cfg.order = batch_order[0]
    first_core = section == 0
    wq = w_qkv[0].transpose(0, 2, 1).reshape(3 * cfg.cols, width)
    wo = w_out[0]
    wq_half, wo_half = 3 * cfg.cols // 2, cfg.cols // 2
    sibling_wq = swap(wq)
    pack = jnp.concatenate([gain_attn, shift_attn, gain_moe, shift_moe, w_router[0].T], axis=0)
    other_pack = swap(pack)
    packs = [
        jnp.where(first_core, pack, other_pack),
        jnp.where(first_core, other_pack, pack),
    ]
    picks = jnp.stack(
        [v[0].reshape(MB, IMG_MB, seq, TOPK)[tensor] for v in (routes, slots)]
    ).transpose(0, 1, 3, 2)
    picks = jnp.pad(picks, ((0, 0), (0, 0), (0, 0), (0, padded - seq)), constant_values=-1)
    picks = picks.reshape(4 * TOPK, padded)
    planned = plan(cfg, picks, swap(picks))
    targets, columns = planned.targets, planned.columns

    def pick(values, index):
        return lax.dynamic_index_in_dim(values, index, 0, keepdims=False)

    weights = [Weights(), Weights()]
    sibling_wo = swap(wo)
    sibling_we = swap(w_back[0])
    wo_own = jnp.where(first_core, wo[:wo_half], sibling_wo[wo_half:])
    weights[0].wo_d = gather_images(wo_own)
    weights[0].wo_f = swaps(weights[0].wo_d)

    def pair(lower, upper):
        return [
            jnp.where(first_core, pick(lower, index), pick(upper, index))
            for index in (local_expert, 1 - local_expert)
        ]

    first_pair = pair(w_in[0], sibling_we)
    weights[0].we_d = relay(*first_pair)
    weights[0].we_f = forward_chunks(weights[0].we_d)
    joined = jnp.where(
        first_core,
        jnp.concatenate([sibling_wq[:wq_half], sibling_wo[:wo_half]], axis=0),
        jnp.concatenate([wq[wq_half:], wo[wo_half:]], axis=0),
    )
    weights[1].wq_d = relay(joined, joined)
    weights[1].wq_f = swaps(weights[1].wq_d)
    sibling_we = swap(w_in[0])
    weights[1].we_d = relay(*pair(sibling_we, w_back[0]))
    weights[1].we_f = forward_chunks(weights[1].we_d)
    wq0_own = jnp.where(first_core, wq[:wq_half], sibling_wq[wq_half:])
    weights[0].wq_d = gather_images(wq0_own)
    weights[0].wq_f = swaps(weights[0].wq_d)

    tokens = lax.optimization_barrier((tokens, *first_pair))[0]
    heads = attention_heads(cfg, tokens, wq, sibling_wq, packs[0])
    rows, saved, arrived_rows, forward = [heads.z], [], [], []
    first = attention_out(cfg, heads.z[0], spread(heads.o), weights[0], packs[0], columns[0])
    saved.append(first)
    sent = dispatch(cfg, first.mm, swap(first.mm), targets[0])
    arrived_rows.append(exchange(cfg, sent))
    other_gates = [swap(first.gates)]
    forward.append(experts_forward(cfg, arrived_rows[0], weights[0]))
    mine = exchange(cfg, forward[0].ye)
    second = combine_attention(
        cfg, mine, swaps(mine), first, columns[0], weights[1], packs[1], columns[1]
    )
    saved.append(second)
    other_gates.append(swap(second.gates))
    rows.append(gather_images(second.out))
    sent = dispatch(cfg, second.mm, swap(second.mm), targets[1])
    arrived_rows.append(exchange(cfg, sent))
    sent = dispatch_back(cfg, cotangent, None, second.gates, other_gates[1], targets[1])
    target_rows = sent.rows
    arrived_grads = [None, exchange(cfg, sent.sent)]
    forward.append(experts_forward(cfg, arrived_rows[1], weights[1]))
    mine = exchange(cfg, forward[1].ye)
    final = last_combine(cfg, mine, swaps(mine), second, columns[1])
    last_rows = relay_images(final.out)
    selected = [second.sel, final.sel]

    grad_rows = [None, None, target_rows]
    expert_grads, parts = [None, None], [None, None]
    for layer in (1, 0):
        if layer == 0:
            sent = dispatch_back(
                cfg, grad_rows[1], swap(grad_rows[1]), first.gates, other_gates[0], targets[0]
            )
            arrived_grads[0] = exchange(cfg, sent.sent)
        back = experts_back(
            cfg,
            arrived_grads[layer],
            forward[layer].x,
            forward[layer].act,
            forward[layer].slope,
            weights[layer],
        )
        mine = exchange(cfg, back.dxe)
        zero, one, two, three = experts_grads(
            cfg,
            forward[layer].x,
            back.x,
            forward[layer].act,
            back.dpre,
            swap(back.rows_out),
            swap(back.hidden),
        )
        three = across(three, 2)
        two = across(two, 2)
        one = add(one, three)
        one = across(one, 1)
        own = add(zero, two)
        expert_grads[layer] = (
            [own, one],
            [swap(own), swap(one)],
        )
        upper = back_to_attention(
            cfg,
            grad_rows[layer + 1],
            saved[layer],
            selected[layer],
            mine,
            swaps(mine),
            packs[layer],
            columns[layer],
        )
        datt = gather_images(upper.datt) if layer == 0 else None
        lower = attention_back(
            cfg, rows[layer][0], saved[layer], upper, weights[layer], packs[layer], layer == 0
        )
        grad_rows[layer] = lower.dz
        sent = spread(lower.sent)
        if layer == 1:
            datt = last_common = relay_images(lower.common)
        grads = attention_grads(
            cfg, rows[layer], sent, datt, heads.o if layer == 0 else None, packs[layer]
        )
        parts[layer] = grads.keep, swap(grads.send)

    split = split_owners(cfg, *zip(*parts))
    split = [split[0]] + [along(split[z], z) for z in range(1, owners)]
    piece = sum_pieces(cfg, split)
    pieces = [piece.total] + [along(piece.total, z) for z in range(1, owners)]

    others = [swaps(rows[1]), swaps(last_rows)]
    acts = place_images(cfg, [rows[1], last_rows], others, (0, 0), LOW)
    first_grads = relay_images(grad_rows[0])
    others = [swaps(first_grads), swaps(last_common)]
    in_grads = place_images(cfg, [first_grads, last_common], others, (0, width), LOW).astype(F32)
    ordered = order_attention_grads(cfg, pieces, piece.small)
    attention_final = place_attention_grads(cfg, ordered.own, swap(ordered.send))
    final_small = ordered.out
    expert_final = place_expert_grads(cfg, *zip(*expert_grads))
    return (
        acts,
        in_grads,
        final_small[experts + 2][None],
        final_small[experts + 3][None],
        attention_final.qkv.transpose(0, 1, 3, 2),
        attention_final.out,
        final_small[experts][None],
        final_small[experts + 1][None],
        final_small[:experts].T[None],
        expert_final.grad_in,
        expert_final.grad_back,
    )


def solution(mesh):
    layered = P(SECTION, None)
    attention = P(SECTION, None, None, TENSOR)
    out = P(SECTION, TENSOR, None)
    experts_in = P(SECTION, EXPERT, None, TENSOR)
    experts_back = P(SECTION, EXPERT, TENSOR, None)
    images = P(SECTION, EXPERT, None, None)
    router = P(SECTION, None, None)
    return jax.shard_map(
        program,
        mesh=mesh,
        in_specs=(
            P(EXPERT, None, None),
            P(EXPERT, None),
            layered,
            layered,
            attention,
            out,
            layered,
            layered,
            router,
            experts_in,
            experts_back,
            images,
            images,
            P(EXPERT, None, None),
        ),
        out_specs=(
            images,
            images,
            layered,
            layered,
            attention,
            out,
            layered,
            layered,
            router,
            experts_in,
            experts_back,
        ),
        check_vma=False,
    )
```
